32 devices in a mesh: group: 2 (over x), section: 4 (over y, core), dp: 4 (over z).
Axes of the slice: x: 2, y: 2, z: 4, core: 2. Of those that a mesh axis runs over, the one named last changes fastest.
Arguments:
- inputs: bfloat16 [4, 256, 1024], P(None, ('group', 'dp')), parts along dimension 1, may hold values from -6 to 6
- cotangent: bfloat16 [4, 256, 1024], P(None, ('group', 'dp')), parts along dimension 1, may hold values from -0.1796875 to 0.1796875
- enc_weights: bfloat16 [4, 1024, 1024], P('section'), may hold values from -0.1875 to 0.1875
- dec_weights: bfloat16 [4, 2048, 1024], P('section'), may hold values from -0.125 to 0.125
Outputs:
- enc_grads: float32 [8, 1024, 1024], P(('group', 'section'), 'dp'), parts along dimension 0
- dec_grads: float32 [8, 2048, 1024], P(('group', 'section'), 'dp'), parts along dimension 0
The draws below stay inside these ranges and needn't reach their ends.
There are 2 independent parts, one for each index of `group`. The reference program is written for one: setup_inputs(seed, part) draws one part's arguments, and reference() takes and returns one part's arrays. A program takes and returns all parts, laid end to end along the dimension named above; an argument that names none is the same for every part. Nothing has to cross between parts.
All inputs are finite; a program needn't handle non-finite values.
Results may differ from the reference program's by a relative error of at most 0.014.
Values may be sent and summed in bfloat16 or wider, within the bound.
No kernel may reach another device: no remote copies, remote signals or barrier semaphores. Data moves between devices by JAX's collectives and lax.ppermute only.
A program may use at most 64 MiB of HBM per device.

```python
import jax
import jax.numpy as jnp
from jax import lax

C = 1024
MB = 4
LEVELS = 4
ROWS = 128


def steps_of(own_key, dims, shards, smallest, high):
    factor_of = 1.0
    for axis_at, shards_of in shards:
        draws = jax.random.uniform(jax.random.fold_in(jax.random.fold_in(own_key, 6), axis_at), (shards_of,), jnp.float32, smallest / len(shards), high / len(shards))
        factor_of = factor_of * jnp.repeat(jnp.exp(draws), dims[axis_at] // shards_of).reshape((-1,) + (1,) * (len(dims) - 1 - axis_at))
    return factor_of


def bell_draw(rng, extent, scale, reach, cuts=(), kind=jnp.bfloat16):
    drawn = jax.random.normal(rng, extent, jnp.float32) * scale
    if len(cuts) > 0:
        drawn = steps_of(rng, extent, cuts, -0.22, 0.18) * drawn
    return jnp.clip(drawn, min=-reach, max=reach).astype(kind)


def setup_inputs(seed: int = 0, part: int = 0) -> dict:
    streams_of = jax.random.split(jax.random.key(seed), 5)
    part_keys = jax.random.split(jax.random.fold_in(streams_of[4], part), 5)
    return {
        "inputs": bell_draw(part_keys[0], (MB, ROWS, C), 1.0, 6.0, ((1, 4),)),
        "cotangent": bell_draw(part_keys[1], (MB, ROWS, C), 0.03, 0.1796875, ((1, 4),)),
        "enc_weights": bell_draw(streams_of[2], (LEVELS, C, C), C ** -0.5, 0.1875, ((0, 4),)),
        "dec_weights": bell_draw(streams_of[3], (LEVELS, 2 * C, C), (2 * C) ** -0.5, 0.125, ((0, 4),)),
    }


EPS = 1e-06

def normalize(values):
    return values * lax.rsqrt(lax.optimization_barrier(jnp.mean(values * values, axis=-1, keepdims=True)) + EPS)

def norm_back(values, grad):
    inv_rms = lax.rsqrt(lax.optimization_barrier(jnp.mean(values * values, axis=-1, keepdims=True)) + EPS)
    normed = values * inv_rms
    return inv_rms * (grad - normed * lax.optimization_barrier(jnp.mean(grad * normed, axis=-1, keepdims=True)))

def silu_grad(pre_act):
    sigma = jax.nn.sigmoid(pre_act)
    return sigma * (1.0 + pre_act * (1.0 - sigma))

def transpose_dot(left, right):
    return lax.dot_general(left, right, (((1,), (1,)), ((), ())), preferred_element_type=jnp.float32)

def row_sum_dot(left, right):
    return lax.dot_general(left, right, (((0,), (0,)), ((), ())), preferred_element_type=jnp.float32)

def encode(hidden, weight):
    values = hidden.astype(jnp.float32)
    normed = normalize(values).astype(jnp.bfloat16)
    pre_act = jnp.dot(normed, weight, preferred_element_type=jnp.float32)
    return (values + jax.nn.silu(pre_act)).astype(jnp.bfloat16)

def decode_mix(state, skip_in):
    both = jnp.concatenate([normalize(state.astype(jnp.float32)), normalize(skip_in.astype(jnp.float32))], axis=-1)
    return both.astype(jnp.bfloat16)

def decode(state, skip_in, weight):
    mixed = decode_mix(state, skip_in)
    pre_act = jnp.dot(mixed, weight, preferred_element_type=jnp.float32)
    return (state.astype(jnp.float32) + jax.nn.silu(pre_act)).astype(jnp.bfloat16)

def encode_back(hidden, weight, grads):
    values = hidden.astype(jnp.float32)
    normed = normalize(values).astype(jnp.bfloat16)
    pre_act = jnp.dot(normed, weight, preferred_element_type=jnp.float32)
    act_grad = (grads.astype(jnp.float32) * silu_grad(pre_act)).astype(jnp.bfloat16)
    norm_grad = transpose_dot(act_grad, weight)
    return grads.astype(jnp.float32) + norm_back(values, norm_grad)

def decode_back(state, skip_in, weight, grads):
    mixed = decode_mix(state, skip_in)
    pre_act = jnp.dot(mixed, weight, preferred_element_type=jnp.float32)
    act_grad = (grads.astype(jnp.float32) * silu_grad(pre_act)).astype(jnp.bfloat16)
    mix_grad = transpose_dot(act_grad, weight)
    channels = state.shape[-1]
    state_grad = grads.astype(jnp.float32) + norm_back(state.astype(jnp.float32), mix_grad[:, :channels])
    skip_grad = norm_back(skip_in.astype(jnp.float32), mix_grad[:, channels:])
    return (state_grad.astype(jnp.bfloat16), skip_grad.astype(jnp.bfloat16))

def encode_wgrad(hidden, weight, grads):
    normed = normalize(hidden.astype(jnp.float32)).astype(jnp.bfloat16)
    pre_act = jnp.dot(normed, weight, preferred_element_type=jnp.float32)
    act_grad = (grads.astype(jnp.float32) * silu_grad(pre_act)).astype(jnp.bfloat16)
    return row_sum_dot(normed, act_grad)

def decode_wgrad(state, skip_in, weight, grads):
    mixed = decode_mix(state, skip_in)
    pre_act = jnp.dot(mixed, weight, preferred_element_type=jnp.float32)
    act_grad = (grads.astype(jnp.float32) * silu_grad(pre_act)).astype(jnp.bfloat16)
    return row_sum_dot(mixed, act_grad)

def reference(inputs, cotangent, enc_weights, dec_weights):
    levels = enc_weights.shape[0]
    channels = enc_weights.shape[1]
    hidden = inputs.reshape(-1, channels)
    skips = []
    for level in range(levels):
        skips.append(hidden)
        hidden = encode(hidden, enc_weights[level])
    state = hidden
    dec_inputs = [None] * levels
    for level in reversed(range(levels)):
        dec_inputs[level] = state
        state = decode(state, skips[level], dec_weights[level])
    grads = cotangent.reshape(-1, channels)
    skip_grads = [None] * levels
    dec_parts = [None] * levels
    for level in range(levels):
        dec_parts[level] = decode_wgrad(dec_inputs[level], skips[level], dec_weights[level], grads)
        grads, skip_grads[level] = decode_back(dec_inputs[level], skips[level], dec_weights[level], grads)
    enc_parts = [None] * levels
    for level in reversed(range(levels)):
        enc_parts[level] = encode_wgrad(skips[level], enc_weights[level], grads)
        summed = encode_back(skips[level], enc_weights[level], grads) + skip_grads[level].astype(jnp.float32)
        grads = summed.astype(jnp.bfloat16)
    return (jnp.stack(enc_parts), jnp.stack(dec_parts))
```

```python
import functools

import jax
import jax.numpy as jnp
from jax import lax
from jax.experimental import pallas as pl
from jax.experimental.pallas import tpu as pltpu
from jax.sharding import PartitionSpec as P

EPS = 1e-06
TILE = 256
VMEM_LIMIT = 58 * 1024 * 1024


def dot(left, right):
    return lax.dot_general(
        left, right, (((1,), (0,)), ((), ())), preferred_element_type=jnp.float32
    )


def dot_t(left, right):
    return lax.dot_general(
        left, right, (((1,), (1,)), ((), ())), preferred_element_type=jnp.float32
    )


def dot_rows(left, right):
    return lax.dot_general(
        left, right, (((0,), (0,)), ((), ())), preferred_element_type=jnp.float32
    )


NEEDS = {
    "enc": (),
    "dec": ("n",),
    "decb": ("n", "r", "nd", "rd", "gb"),
    "encb": ("n", "r", "ga", "k"),
}
MAKES = {
    "enc": ("n", "r", "ga"),
    "dec": ("nd", "rd", "gb"),
    "decb": ("k",),
    "encb": (),
}
SENDS = {"enc": ("nc",), "dec": ("mc",), "decb": ("u",), "encb": ("e",)}


def stage_kernel(cfg, *refs):
    ops, pair, wide, last, blocks, names = (
        cfg["ops"], cfg["pair"], cfg["wide"], cfg["last"], cfg["blocks"], cfg["names"]
    )
    ref = dict(zip(names, refs))
    sems = ref["sems"]
    section = lax.axis_index("section")
    core = lax.rem(section, 2)
    live = True if pair is None else lax.div(section, 2) == pair
    dp = lax.axis_index("dp")
    dp_count = cfg["dp_count"]
    x, ybuf = ref["v_x"], ref["v_y"]
    rows, channels = x.shape
    block_rows = rows // blocks
    tile_count = channels // TILE

    def for_tiles(step, carry=0):
        def run(j, carry):
            at = j * TILE
            if not isinstance(j, int):
                at = pl.multiple_of(at, TILE)
            return step(at, pl.ds(at, TILE), carry)

        if cfg["unroll"]:
            for j in range(tile_count):
                carry = run(j, carry)
            return carry
        return lax.fori_loop(0, tile_count, run, carry)

    def run_live():
        counter = [0]
        waits = {}

        def start(key, source, target):
            copy = pltpu.make_async_copy(source, target, sems.at[counter[0]])
            counter[0] += 1
            copy.start()
            waits.setdefault(key, []).append(copy)

        def ready(key):
            for copy in waits.pop(key, []):
                copy.wait()

        for b in range(blocks):
            start("x", ref["x%d" % b], x.at[pl.ds(b * block_rows, block_rows)])
        made = set()
        for op in ops:
            for name in NEEDS[op]:
                if name not in made and not (name in ("n", "r") and last and not wide and op == "decb"):
                    if name not in waits:
                        start(name, ref[name], ref["v_" + name])
            made.update(MAKES[op])
            kind = "we" if op in ("enc", "encb") else "wd"
            if kind not in waits:
                start(kind, ref[kind + "_own"], ref["v_" + kind].at[core])
                start(kind, ref[kind + "_oth"], ref["v_" + kind].at[1 - core])
            if op == "decb" and "dec" in ops:
                for b in range(blocks):
                    start("q", ref["q%d" % b], ref["v_q"].at[pl.ds(b * block_rows, block_rows)])

        outs = []

        def store(source, target):
            copy = pltpu.make_async_copy(source, target, sems.at[counter[0]])
            counter[0] += 1
            copy.start()
            outs.append(copy)

        def store_split(level, source, name):
            sem = sems.at[counter[0]]
            counter[0] += 1

            @pl.when(core == level)
            def _():
                pltpu.make_async_copy(source, ref[name + "_own"], sem).start()

            @pl.when(core != level)
            def _():
                pltpu.make_async_copy(source, ref[name + "_send"], sem).start()

            outs.append(pltpu.make_async_copy(source, ref[name + "_own"], sem))

        def normalize(level, n_ref, r_ref):
            values = x[...].astype(jnp.float32)
            inv = lax.rsqrt(jnp.mean(values * values, axis=-1, keepdims=True) + EPS)
            n_ref[level] = (values * inv).astype(jnp.bfloat16)
            r_ref[level] = jnp.broadcast_to(inv, (rows, 128))

        def activate(pre, gain_ref, level, sl):
            sigma = jax.nn.sigmoid(pre)
            gain_ref[level, :, sl] = sigma * (1.0 + pre * (1.0 - sigma))
            x[:, sl] = (x[:, sl].astype(jnp.float32) + pre * sigma).astype(jnp.bfloat16)

        def enc_level(level):
            n, we = ref["v_n"], ref["v_we"]
            normalize(level, n, ref["v_r"])
            ready("we")

            def step(at, sl, carry):
                activate(dot(n[level], we[level, :, sl]), ref["v_ga"], level, sl)
                return carry

            for_tiles(step)
            if wide:
                width = channels // dp_count
                at = pl.multiple_of(dp * width, 128)
                store_split(level, n.at[level, :, pl.ds(at, width)], "nc")

        def dec_level(level):
            n, nd, wd = ref["v_n"], ref["v_nd"], ref["v_wd"]
            normalize(level, nd, ref["v_rd"])
            ready("n")
            ready("wd")

            def step(at, sl, carry):
                pre = dot(nd[level], wd[level, :channels, sl]) + dot(
                    n[level], wd[level, channels:, sl]
                )
                activate(pre, ref["v_gb"], level, sl)
                return carry

            for_tiles(step)
            if wide:
                width = 2 * channels // dp_count
                half = dp_count // 2
                sem = sems.at[counter[0]]
                counter[0] += 1
                for is_skip, buf in ((0, nd), (1, n)):
                    index = jnp.maximum(dp - half, 0) if is_skip else jnp.minimum(dp, half - 1)
                    source = buf.at[level, :, pl.ds(pl.multiple_of(index * width, 128), width)]
                    mine = (dp >= half) if is_skip else (dp < half)

                    @pl.when(mine & (core == level))
                    def _():
                        pltpu.make_async_copy(source, ref["mc_own"], sem).start()

                    @pl.when(mine & (core != level))
                    def _():
                        pltpu.make_async_copy(source, ref["mc_send"], sem).start()

                outs.append(pltpu.make_async_copy(nd.at[level, :, pl.ds(0, width)], ref["mc_own"], sem))

        def back(grad_ref, level, w_ref, base, n_ref, finish):
            grad = grad_ref[level]

            def step(at, sl, total):
                part = dot_t(grad, w_ref[level, pl.ds(base + at, TILE), :])
                ybuf[:, sl] = part
                return total + jnp.sum(
                    part * n_ref[level, :, sl].astype(jnp.float32), axis=-1, keepdims=True
                )

            total = for_tiles(step, jnp.zeros((rows, 1), jnp.float32)) / channels

            def close(at, sl, carry):
                finish(sl, ybuf[:, sl] - n_ref[level, :, sl].astype(jnp.float32) * total)
                return carry

            for_tiles(close)

        def decb_level(level):
            n, nd, wd, u, k = ref["v_n"], ref["v_nd"], ref["v_wd"], ref["v_u"], ref["v_k"]
            ready("gb")
            u[level] = (x[...].astype(jnp.float32) * ref["v_gb"][level]).astype(jnp.bfloat16)
            if wide:
                store_split(level, u.at[level], "u")
            ready("nd")
            ready("rd")
            ready("wd")
            rd = ref["v_rd"][level, :, :1]

            def finish(sl, value):
                x[:, sl] = (x[:, sl].astype(jnp.float32) + rd * value).astype(jnp.bfloat16)

            if not (wide and level == 1 and ops[-1] == "decb"):
                back(u, level, wd, 0, nd, finish)
            if wide or not last:
                ready("n")
                ready("r")
                r = ref["v_r"][level, :, :1]

                def finish_skip(sl, value):
                    k[level, :, sl] = (r * value).astype(jnp.bfloat16)

                back(u, level, wd, channels, n, finish_skip)

        def encb_level(level):
            n, we, e, k = ref["v_n"], ref["v_we"], ref["v_e"], ref["v_k"]
            ready("ga")
            e[level] = (x[...].astype(jnp.float32) * ref["v_ga"][level]).astype(jnp.bfloat16)
            if wide:
                store_split(level, e.at[level], "e")
            if wide and level == 0:
                return
            ready("we")
            ready("n")
            ready("r")
            ready("k")
            r = ref["v_r"][level, :, :1]

            def finish(sl, value):
                x[:, sl] = (
                    x[:, sl].astype(jnp.float32) + r * value + k[level, :, sl].astype(jnp.float32)
                ).astype(jnp.bfloat16)

            back(e, level, we, 0, n, finish)

        ready("x")
        for op in ops:
            if op == "enc":
                enc_level(0)
                enc_level(1)
            if op == "dec":
                dec_level(1)
                dec_level(0)
            if op == "decb":
                if "dec" in ops:
                    ready("q")
                    x[...] = ref["v_q"][...]
                decb_level(0)
                decb_level(1)
            if op == "encb":
                encb_level(1)
                encb_level(0)
            if not wide and op == ops[-1]:
                store(x, ref["out_x"])
            for name in MAKES[op]:
                if name == "k" and ("encb" in ops or (last and not wide)):
                    continue
                store(ref["v_" + name], ref["out_" + name])
        for key in list(waits):
            ready(key)
        for copy in outs:
            copy.wait()

    if pair is None:
        run_live()
    else:
        pl.when(live)(run_live)


def run_stage(ops, pair, wide, pairs, xs, qs, weights, state, dp_count, after=()):
    block_rows, channels = xs[0].shape
    blocks = len(xs)
    rows = block_rows * blocks
    last = pair == 0
    bf16, f32 = jnp.bfloat16, jnp.float32
    kinds = {
        "n": ((2, rows, channels), bf16), "r": ((2, rows, 128), f32), "ga": ((2, rows, channels), f32),
        "nd": ((2, rows, channels), bf16), "rd": ((2, rows, 128), f32), "gb": ((2, rows, channels), f32),
        "k": ((2, rows, channels), bf16),
        "nc": ((rows, channels // dp_count), bf16), "mc": ((rows, 2 * channels // dp_count), bf16),
        "u": ((rows, channels), bf16), "e": ((rows, channels), bf16),
    }
    names, args = [], []
    for b, value in enumerate(xs):
        names.append("x%d" % b)
        args.append(value)
    if "dec" in ops and "decb" in ops:
        for b, value in enumerate(qs):
            names.append("q%d" % b)
            args.append(value)
    for kind, users in (("we", ("enc", "encb")), ("wd", ("dec", "decb"))):
        if any(op in users for op in ops):
            names += [kind + "_own", kind + "_oth"]
            args += list(weights[kind])
    made = set()
    for op in ops:
        for name in NEEDS[op]:
            if name not in made and name not in names:
                if name == "k" and "decb" in ops:
                    continue
                names.append(name)
                args.append(state[name])
        made.update(MAKES[op])
    for i, value in enumerate(after):
        names.append("after%d" % i)
        args.append(value)
    outs = []
    if not wide:
        outs.append(("out_x", None, ((rows, channels), bf16)))
    for op in ops:
        for name in MAKES[op]:
            if name == "k" and ("encb" in ops or (last and not wide)):
                continue
            outs.append(("out_" + name, name, kinds[name]))
        if wide:
            for name in SENDS[op]:
                for tail in ("_own", "_send"):
                    outs.append((name + tail, name + tail, kinds[name]))
    aliases = {}
    for i, (_, key, _) in enumerate(outs):
        if key is not None and key in state:
            if key in names:
                aliases[names.index(key)] = i
            else:
                aliases[len(args)] = i
                names.append("prior_" + key)
                args.append(state[key])
    in_count = len(args)
    names += [o[0] for o in outs]
    scratch = {"v_x": ((rows, channels), bf16), "v_y": ((rows, channels), f32)}
    if "dec" in ops and "decb" in ops:
        scratch["v_q"] = ((rows, channels), bf16)
    for op in ops:
        for name in NEEDS[op] + MAKES[op]:
            scratch["v_" + name] = kinds[name]
        if op in ("enc", "encb"):
            scratch["v_we"] = ((2, channels, channels), bf16)
        else:
            scratch["v_wd"] = ((2, 2 * channels, channels), bf16)
        if op == "decb":
            scratch["v_u"] = ((2, rows, channels), bf16)
        if op == "encb":
            scratch["v_e"] = ((2, rows, channels), bf16)
    names += list(scratch) + ["sems"]
    cfg = dict(ops=ops, pair=pair, wide=wide, last=last, blocks=blocks, names=names, dp_count=dp_count,
               unroll=pairs <= 2)
    any_spec = pl.BlockSpec(memory_space=pl.ANY)
    flops = 2 * rows * channels * channels * 4 * len(ops)
    results = pl.pallas_call(
        functools.partial(stage_kernel, cfg),
        name=("wide_" if wide else "chain_") + "_".join(ops),
        out_shape=[jax.ShapeDtypeStruct(*o[2]) for o in outs],
        in_specs=[any_spec] * in_count,
        out_specs=[any_spec] * len(outs),
        scratch_shapes=[pltpu.VMEM(*s) for s in scratch.values()] + [pltpu.SemaphoreType.DMA((64,))],
        input_output_aliases=aliases,
        compiler_params=pltpu.CompilerParams(vmem_limit_bytes=VMEM_LIMIT),
        cost_estimate=pl.CostEstimate(
            flops=flops, bytes_accessed=8 * 1024 * 1024, transcendentals=0
        ),
    )(*args)
    state = dict(state)
    x_out = None
    for (name, key, _), value in zip(outs, results):
        if key is None:
            x_out = value
        else:
            state[key] = value
    return x_out, state


def wgrad_kernel(a_own, a_oth, b_own, b_oth, out):
    for j in range(0, out.shape[1], TILE):
        sl = slice(j, j + TILE)
        out[:, sl] = dot_rows(a_own[...], b_own[:, sl]) + dot_rows(a_oth[...], b_oth[:, sl])


def wgrad(a_own, a_oth, b_own, b_oth):
    width, channels = a_own.shape[1], b_own.shape[1]
    vmem = pl.BlockSpec(memory_space=pltpu.VMEM)
    return pl.pallas_call(
        wgrad_kernel,
        out_shape=jax.ShapeDtypeStruct((width, channels), jnp.float32),
        in_specs=[vmem] * 4,
        out_specs=vmem,
        compiler_params=pltpu.CompilerParams(vmem_limit_bytes=VMEM_LIMIT),
        cost_estimate=pl.CostEstimate(
            flops=4 * a_own.shape[0] * width * channels, bytes_accessed=4 * 1024 * 1024, transcendentals=0
        ),
    )(a_own, a_oth, b_own, b_oth)


def body(inputs, cotangent, enc_weights, dec_weights):
    section_count = lax.axis_size("section")
    dp_count = lax.axis_size("dp")
    core = lax.rem(lax.axis_index("section"), 2)
    pairs = section_count // 2
    batches, row_count, channels = inputs.shape
    half = batches * row_count // 2

    def my_rows(values):
        flat = values.reshape(2, half, channels)
        return lax.dynamic_index_in_dim(flat, core, 0, keepdims=False)

    def swap(value):
        return lax.ppermute(value, "section", [(i, i ^ 1) for i in range(section_count)])

    def over_dp(value):
        return [value] + [
            lax.ppermute(value, "dp", [(i, (i + k) % dp_count) for i in range(dp_count)])
            for k in range(1, dp_count)
        ]

    def hop(value, source, target, reach):
        return [
            lax.ppermute(
                value,
                ("section", "dp"),
                [
                    ((2 * source + c) * dp_count + d, (2 * target + c) * dp_count + (d + k) % dp_count)
                    for c in range(2)
                    for d in range(dp_count)
                ],
            )
            for k in range(reach)
        ]

    we, wd = enc_weights[0], dec_weights[0]
    weights = {"we": (we, swap(we)), "wd": (wd, swap(wd))}
    x0, cot = my_rows(inputs), my_rows(cotangent)
    x_all, cot_all = (over_dp(x0), over_dp(cot)) if pairs <= 2 else ([], [])

    visits = [("enc", k) for k in range(pairs)]
    visits += [("dec", k) for k in reversed(range(pairs))]
    visits += [("decb", k) for k in range(pairs)]
    visits += [("encb", k) for k in reversed(range(pairs))]
    stages = []
    for op, k in visits:
        if pairs <= 2 and stages and stages[-1][1] == k:
            stages[-1] = (stages[-1][0] + (op,), k)
        else:
            stages.append(((op,), k))

    chain, wide = {}, {}
    if pairs <= 2:
        arrived, waiting = x_all, None
        for i, (ops, k) in enumerate(stages[:-1]):
            x_out, chain = run_stage(
                ops, k, False, pairs, arrived[:1], [cot], weights, chain, dp_count
            )
            if waiting is not None:
                w_ops, w_k, w_x = waiting
                _, wide = run_stage(
                    w_ops, w_k, True, pairs, w_x, cot_all, weights, wide, dp_count, after=(x_out,)
                )
            waiting = (ops, k, arrived)
            arrived = hop(x_out, k, stages[i + 1][1], dp_count)
        for w_ops, w_k, w_x in (waiting, stages[-1] + (arrived,)):
            _, wide = run_stage(w_ops, w_k, True, pairs, w_x, cot_all, weights, wide, dp_count)
    else:
        my_pair = lax.div(lax.axis_index("section"), 2)
        arrived = x0
        for i, (ops, k) in enumerate(stages):
            if i % pairs == 0:
                entry = arrived
            else:
                entry = jnp.where(my_pair == k, arrived, entry)
            if i % pairs == pairs - 1:
                _, wide = run_stage(
                    ops, None, True, pairs, over_dp(entry), [], weights, wide, dp_count
                )
            if i == len(stages) - 1:
                break
            x_out, chain = run_stage(ops, k, False, pairs, [arrived], [], weights, chain, dp_count)
            target = stages[i + 1][1]
            if stages[i + 1] == (("decb",), 0):
                arrived = cot
            elif target == k:
                arrived = x_out
            else:
                arrived = hop(x_out, k, target, 1)[0]

    other = {name: swap(wide[name + "_send"]) for name in ("nc", "mc", "u", "e")}
    enc_grads = wgrad(wide["nc_own"], other["nc"], wide["e_own"], other["e"])
    dec_grads = wgrad(wide["mc_own"], other["mc"], wide["u_own"], other["u"])
    return (enc_grads[None], dec_grads[None])


def solution(mesh):
    in_specs = (
        P(None, ("group", "dp"), None),
        P(None, ("group", "dp"), None),
        P("section", None, None),
        P("section", None, None),
    )
    out_specs = (P(("group", "section"), "dp", None), P(("group", "section"), "dp", None))
    return jax.shard_map(body, mesh=mesh, in_specs=in_specs, out_specs=out_specs, check_vma=False)
```

```python
import functools

import jax
import jax.numpy as jnp
from jax import lax
from jax.experimental import pallas as pl
from jax.experimental.pallas import tpu as pltpu
from jax.sharding import PartitionSpec as P

EPS = 1e-06
TILE = 256
VMEM_LIMIT = 22 * 1024 * 1024
WIDE_LIMIT = 40 * 1024 * 1024


def dot(left, right):
    return lax.dot_general(
        left, right, (((1,), (0,)), ((), ())), preferred_element_type=jnp.float32
    )


def dot_t(left, right):
    return lax.dot_general(
        left, right, (((1,), (1,)), ((), ())), preferred_element_type=jnp.float32
    )


def dot_rows(left, right):
    return lax.dot_general(
        left, right, (((0,), (0,)), ((), ())), preferred_element_type=jnp.float32
    )


NEEDS = {
    "enc": (),
    "dec": ("n",),
    "decb": ("n", "r", "nd", "rd", "gb"),
    "encb": ("n", "r", "ga", "k"),
}
MAKES = {
    "enc": ("n", "r", "ga"),
    "dec": ("nd", "rd", "gb"),
    "decb": ("k",),
    "encb": (),
}
VMEM = pl.BlockSpec(memory_space=pltpu.VMEM)
ANY = pl.BlockSpec(memory_space=pl.ANY)


def own_kernel(own, both, sem):
    core = lax.rem(lax.axis_index("section"), 2)
    copy = pltpu.make_async_copy(own, both.at[core], sem)
    copy.start()
    copy.wait()


def other_kernel(before, other, both, sem):
    core = lax.rem(lax.axis_index("section"), 2)
    copy = pltpu.make_async_copy(other, both.at[1 - core], sem)
    copy.start()
    copy.wait()


def load_own(own):
    return pl.pallas_call(
        own_kernel,
        name="load_own",
        out_shape=jax.ShapeDtypeStruct((2,) + own.shape, own.dtype),
        in_specs=[pl.BlockSpec(memory_space=pltpu.HBM)],
        out_specs=VMEM,
        scratch_shapes=[pltpu.SemaphoreType.DMA],
        compiler_params=pltpu.CompilerParams(vmem_limit_bytes=VMEM_LIMIT),
    )(own)


def load_other(both, other):
    return pl.pallas_call(
        other_kernel,
        name="load_other",
        out_shape=jax.ShapeDtypeStruct(both.shape, both.dtype),
        in_specs=[VMEM, ANY],
        out_specs=VMEM,
        input_output_aliases={0: 0},
        scratch_shapes=[pltpu.SemaphoreType.DMA],
        compiler_params=pltpu.CompilerParams(vmem_limit_bytes=VMEM_LIMIT),
    )(both, other)


def stage_kernel(cfg, *refs):
    ops, pair, wide, dp_count = cfg["ops"], cfg["pair"], cfg["wide"], cfg["dp_count"]
    ref = dict(zip(cfg["names"], refs))
    section = lax.axis_index("section")
    core = lax.rem(section, 2)
    dp = lax.axis_index("dp")
    x = ref["out_x"] if "out_x" in ref else ref["work_x"]
    ybuf = ref.get("ybuf")
    rows, channels = x.shape
    tile_count = channels // TILE
    skip_k = cfg["skip_k"]

    def for_tiles(step, carry=0):
        def run(j, carry):
            at = j * TILE
            if not isinstance(j, int):
                at = pl.multiple_of(at, TILE)
            return step(at, pl.ds(at, TILE), carry)

        if cfg["unroll"]:
            for j in range(tile_count):
                carry = run(j, carry)
            return carry
        return lax.fori_loop(0, tile_count, run, carry)

    def by_core(level, name, cols, value):
        @pl.when(core == level)
        def _():
            ref[name + "_own"][:, cols] = value

        @pl.when(core != level)
        def _():
            ref[name + "_send"][:, cols] = value

    def normalize(level, n_ref, r_ref):
        values = x[...].astype(jnp.float32)
        inv = lax.rsqrt(jnp.mean(values * values, axis=-1, keepdims=True) + EPS)
        n_ref[level] = (values * inv).astype(jnp.bfloat16)
        r_ref[level] = jnp.broadcast_to(inv, (rows, 128))

    def activate(pre, gain_ref, level, sl):
        sigma = jax.nn.sigmoid(pre)
        gain_ref[level, :, sl] = sigma * (1.0 + pre * (1.0 - sigma))
        x[:, sl] = (x[:, sl].astype(jnp.float32) + pre * sigma).astype(jnp.bfloat16)

    def enc_level(level):
        n, we = ref["n"], ref["we"]
        normalize(level, n, ref["r"])

        def step(at, sl, carry):
            activate(dot(n[level], we[level, :, sl]), ref["ga"], level, sl)
            return carry

        for_tiles(step)

    def dec_level(level):
        n, nd, wd = ref["n"], ref["nd"], ref["wd"]
        normalize(level, nd, ref["rd"])

        def step(at, sl, carry):
            pre = dot(nd[level], wd[level, :channels, sl]) + dot(n[level], wd[level, channels:, sl])
            activate(pre, ref["gb"], level, sl)
            return carry

        for_tiles(step)

    def back(grad_ref, level, w_ref, base, n_ref, finish):
        grad = grad_ref[level]

        def step(at, sl, total):
            part = dot_t(grad, w_ref[level, pl.ds(base + at, TILE), :])
            ybuf[:, sl] = part
            return total + jnp.sum(
                part * n_ref[level, :, sl].astype(jnp.float32), axis=-1, keepdims=True
            )

        total = for_tiles(step, jnp.zeros((rows, 1), jnp.float32)) / channels

        def close(at, sl, carry):
            finish(sl, ybuf[:, sl] - n_ref[level, :, sl].astype(jnp.float32) * total)
            return carry

        for_tiles(close)

    def decb_level(level):
        n, nd, wd, u = ref.get("n"), ref["nd"], ref["wd"], ref["u"]
        u[level] = (x[...].astype(jnp.float32) * ref["gb"][level]).astype(jnp.bfloat16)
        if wide:
            width = channels // dp_count
            half = dp_count // 2
            by_core(
                level, "p", pl.ds(0, width),
                n[level, :, pl.ds(pl.multiple_of(dp * width, 128), width)],
            )
            low = pl.multiple_of(jnp.minimum(dp, half - 1) * 2 * width, 128)
            high = pl.multiple_of(jnp.maximum(dp - half, 0) * 2 * width, 128)

            @pl.when(dp < half)
            def _():
                by_core(level, "p", pl.ds(width, 2 * width), nd[level, :, pl.ds(low, 2 * width)])

            @pl.when(dp >= half)
            def _():
                by_core(level, "p", pl.ds(width, 2 * width), n[level, :, pl.ds(high, 2 * width)])

            by_core(level, "p", pl.ds(3 * width, channels), u[level])
        rd = ref["rd"][level, :, :1]

        def finish(sl, value):
            x[:, sl] = (x[:, sl].astype(jnp.float32) + rd * value).astype(jnp.bfloat16)

        if not (wide and level == 1 and ops[-1] == "decb"):
            back(u, level, wd, 0, nd, finish)
        if not skip_k:
            r, k = ref["r"][level, :, :1], ref["k"]

            def finish_skip(sl, value):
                k[level, :, sl] = (r * value).astype(jnp.bfloat16)

            back(u, level, wd, channels, n, finish_skip)

    def encb_level(level):
        n, we, e, k = ref["n"], ref["we"], ref["e"], ref["k"]
        e[level] = (x[...].astype(jnp.float32) * ref["ga"][level]).astype(jnp.bfloat16)
        if wide:
            by_core(level, "e", slice(None), e[level])
        if wide and level == 0:
            return
        r = ref["r"][level, :, :1]

        def finish(sl, value):
            x[:, sl] = (
                x[:, sl].astype(jnp.float32) + r * value + k[level, :, sl].astype(jnp.float32)
            ).astype(jnp.bfloat16)

        back(e, level, we, 0, n, finish)

    def fill(layout):
        for name, offset, flip in layout:
            source = ref[name]
            if flip is None:
                x[...] = source[offset : offset + rows]
            else:
                size = rows // dp_count
                at = pl.multiple_of(lax.bitwise_xor(dp, flip) * size, size)
                x[pl.ds(at, size)] = source[offset : offset + size]

    def run_live():
        fill(cfg["x_layout"])
        for op in ops:
            if op == "enc":
                enc_level(0)
                enc_level(1)
            if op == "dec":
                dec_level(1)
                dec_level(0)
            if op == "decb":
                if "dec" in ops:
                    fill(cfg["q_layout"])
                decb_level(0)
                decb_level(1)
            if op == "encb":
                encb_level(1)
                encb_level(0)

    if pair is None:
        run_live()
    else:
        here = lax.div(section, 2) == pair
        pl.when(here)(run_live)
        if cfg["prior"]:

            @pl.when(jnp.logical_not(here))
            def _():
                for name in cfg["prior"]:
                    ref[name][...] = ref["prior_" + name][...]


def run_stage(ops, pair, wide, unroll, rows, xs, qs, weights, state, dp_count, prior=()):
    channels = xs[0][0].shape[1]
    skip_k = pair == 0 and not wide
    bf16, f32 = jnp.bfloat16, jnp.float32
    matrix, pile = ((rows, channels), bf16), ((2, rows, channels), bf16)
    kinds = {
        "n": pile, "nd": pile, "k": pile, "u": pile, "e": pile,
        "r": ((2, rows, 128), f32), "rd": ((2, rows, 128), f32),
        "ga": ((2, rows, channels), f32), "gb": ((2, rows, channels), f32),
        "p": ((rows, channels + 3 * channels // dp_count), bf16),
    }
    names, args = [], []

    def operands(blocks):
        layout = []
        for value, offset, flip in blocks:
            known = [i for i, arg in enumerate(args) if arg is value]
            if known:
                name = names[known[0]]
            else:
                name = "x%d" % len(args)
                names.append(name)
                args.append(value)
            layout.append((name, offset, flip))
        return tuple(layout)

    x_layout = operands(xs)
    q_layout = operands(qs) if "dec" in ops and "decb" in ops else ()
    for kind, users in (("we", ("enc", "encb")), ("wd", ("dec", "decb"))):
        if any(op in users for op in ops):
            names.append(kind)
            args.append(weights[kind])
    made = set()
    for op in ops:
        for name in NEEDS[op]:
            if name not in made and name not in names and not (skip_k and op == "decb" and name in ("n", "r")):
                names.append(name)
                args.append(state[name])
        made.update(MAKES[op])
    for name in prior:
        names.append("prior_" + name)
        args.append(prior[name])
    in_count = len(args)
    outs, scratch = [], {}
    if not wide:
        outs.append(("out_x", matrix))
    else:
        scratch["work_x"] = matrix
    for op in ops:
        for name in MAKES[op]:
            if name == "k" and skip_k:
                continue
            if (name == "k" and "encb" in ops) or (name in ("nd", "rd", "gb") and "decb" in ops):
                scratch[name] = kinds[name]
            else:
                outs.append((name, kinds[name]))
        if op == "decb":
            scratch["u"] = pile
            if wide:
                outs += [("p_own", kinds["p"]), ("p_send", kinds["p"])]
        if op == "encb":
            scratch["e"] = pile
            if wide:
                outs += [("e_own", matrix), ("e_send", matrix)]
    if "decb" in ops or "encb" in ops:
        scratch["ybuf"] = ((rows, channels), f32)
    names += [o[0] for o in outs] + list(scratch)
    cfg = dict(
        ops=ops, pair=pair, wide=wide, names=names, dp_count=dp_count, skip_k=skip_k,
        unroll=unroll, prior=tuple(prior), x_layout=x_layout, q_layout=q_layout,
    )
    results = pl.pallas_call(
        functools.partial(stage_kernel, cfg),
        name=("wide_" if wide else "chain_") + "_".join(ops),
        out_shape=[jax.ShapeDtypeStruct(*o[1]) for o in outs],
        in_specs=[VMEM] * in_count,
        out_specs=[VMEM] * len(outs),
        scratch_shapes=[pltpu.VMEM(*v) for v in scratch.values()],
        compiler_params=pltpu.CompilerParams(
            vmem_limit_bytes=VMEM_LIMIT if unroll else WIDE_LIMIT
        ),
        cost_estimate=pl.CostEstimate(
            flops=1024, bytes_accessed=1024, transcendentals=0,
        ),
    )(*args)
    made = {name: value for (name, _), value in zip(outs, results)}
    x_out = made.pop("out_x", None)
    return x_out, {**state, **made}


def wgrad_kernel(skip, base, a_own, a_oth, b_own, b_oth, out, buf, sems):
    width, channels = buf.shape
    copies = []
    for index in range(channels // TILE):
        at = index * TILE
        total = dot_rows(a_own[:, skip : skip + width], b_own[:, base + at : base + at + TILE])
        total += dot_rows(a_oth[:, skip : skip + width], b_oth[:, base + at : base + at + TILE])
        buf[:, at : at + TILE] = total
        copy = pltpu.make_async_copy(
            buf.at[:, pl.ds(at, TILE)], out.at[:, pl.ds(at, TILE)], sems.at[index]
        )
        copy.start()
        copies.append(copy)
    for copy in copies:
        copy.wait()


def wgrad(name, skip, width, base, channels, a_own, a_oth, b_own, b_oth):
    return pl.pallas_call(
        functools.partial(wgrad_kernel, skip, base),
        name=name,
        out_shape=jax.ShapeDtypeStruct((width, channels), jnp.float32),
        in_specs=[VMEM] * 4,
        out_specs=ANY,
        scratch_shapes=[
            pltpu.VMEM((width, channels), jnp.float32),
            pltpu.SemaphoreType.DMA((channels // TILE,)),
        ],
        compiler_params=pltpu.CompilerParams(vmem_limit_bytes=VMEM_LIMIT),
        cost_estimate=pl.CostEstimate(
            flops=1024, bytes_accessed=1024, transcendentals=0,
        ),
    )(a_own, a_oth, b_own, b_oth)


def pack_kernel(inputs, cotangent, out, sems):
    core = lax.rem(lax.axis_index("section"), 2)
    count, row_count = inputs.shape[0] // 2, inputs.shape[1]
    copies = []
    for index, source in enumerate((inputs, cotangent)):
        for b in range(count):
            slot = index * count + b
            copies.append(
                pltpu.make_async_copy(
                    source.at[core * count + b],
                    out.at[pl.ds(slot * row_count, row_count)],
                    sems.at[slot],
                )
            )
            copies[-1].start()
    for copy in copies:
        copy.wait()


def pack(inputs, cotangent):
    batches, row_count, channels = inputs.shape
    return pl.pallas_call(
        pack_kernel,
        name="pack",
        out_shape=jax.ShapeDtypeStruct((batches * row_count, channels), inputs.dtype),
        in_specs=[pl.BlockSpec(memory_space=pltpu.HBM)] * 2,
        out_specs=VMEM,
        scratch_shapes=[pltpu.SemaphoreType.DMA((batches,))],
        compiler_params=pltpu.CompilerParams(vmem_limit_bytes=VMEM_LIMIT),
    )(inputs, cotangent)


def merge_kernel(low_count, *refs):
    pair = lax.div(lax.axis_index("section"), 2)
    out = refs[-1]
    for index, sources in enumerate((refs[:low_count], refs[low_count:-1])):

        @pl.when(pair == index)
        def _():
            at = 0
            for source in sources:
                size = source.shape[0]
                out[at : at + size] = source[...]
                at += size


def merge(low, high):
    rows = sum(value.shape[0] for value in low)
    return pl.pallas_call(
        functools.partial(merge_kernel, len(low)),
        name="merge",
        out_shape=jax.ShapeDtypeStruct((rows, low[0].shape[1]), low[0].dtype),
        in_specs=[VMEM] * (len(low) + len(high)),
        out_specs=VMEM,
        compiler_params=pltpu.CompilerParams(vmem_limit_bytes=VMEM_LIMIT),
    )(*low, *high)


def after(value, *others):
    return lax.optimization_barrier((value,) + others)[0]


def body(inputs, cotangent, enc_weights, dec_weights):
    section_count = lax.axis_size("section")
    dp_count = lax.axis_size("dp")
    core = lax.rem(lax.axis_index("section"), 2)
    pairs = section_count // 2
    batches, row_count, channels = inputs.shape
    half = batches * row_count // 2

    def my_rows(values):
        flat = values.reshape(2, half, channels)
        return lax.dynamic_index_in_dim(flat, core, 0, keepdims=False)

    def swap(value):
        return lax.ppermute(value, "section", [(i, i ^ 1) for i in range(section_count)])

    def flip_dp(value, flip, only=None):
        if only is None:
            return lax.ppermute(value, "dp", [(i, i ^ flip) for i in range(dp_count)])
        first = 2 * only * dp_count
        return lax.ppermute(
            value, ("section", "dp"), [(first + i, first + (i ^ flip)) for i in range(2 * dp_count)]
        )

    def over_dp(value):
        return lax.all_gather(value, "dp", axis=0, tiled=True)

    def hop(value, source, target, flips=(0,)):
        return [
            lax.ppermute(
                value,
                ("section", "dp"),
                [
                    ((2 * source + c) * dp_count + d, (2 * target + c) * dp_count + (d ^ flip))
                    for c in range(2)
                    for d in range(dp_count)
                ],
            )
            for flip in flips
        ]

    we, wd = enc_weights[0], dec_weights[0]
    we_other = swap(we)

    def stage(ops, k, wide, xs, qs, weights, state, prior=(), rows=half):
        return run_stage(
            ops, k, wide, pairs <= 2, rows, xs, qs, weights, state, dp_count, prior
        )

    if pairs == 2 and dp_count == 4:
        wide_rows = half * dp_count
        packed = pack(inputs, cotangent)
        packed_two = flip_dp(packed, 2)
        wd_other = swap(after(wd, we_other, packed))
        weights = {"we": load_other(load_own(we), we_other), "wd": load_other(load_own(wd), wd_other)}
        h_top, low = stage(("enc",), 0, False, [(packed, 0, None)], [], weights, {})
        h_in, h_two = hop(h_top, 0, 1, (0, 2))
        d_top, high = stage(("enc", "dec"), 1, False, [(h_in, 0, None)], [], weights, {})
        d_in, d_two = hop(d_top, 1, 0, (0, 2))
        near = flip_dp(
            merge([packed, packed_two], [h_in, after(h_two, d_top), h_in, h_two]), 1
        )
        q_top, low = stage(
            ("dec", "decb"), 0, False, [(d_in, 0, None)], [(packed, half, None)], weights, low
        )
        q_in, q_two = hop(q_top, 0, 1, (0, 2))
        d_both = merge([d_in, d_two], [d_in, d_two])
        d_near = flip_dp(d_both, 1, 0)
        p_top, high = stage(
            ("decb", "encb"), 1, False, [(after(q_in, d_both), 0, None)], [], weights, high
        )
        q_late = after(q_two, p_top)
        q_near = flip_dp(merge([q_in, q_late], [q_in, q_late]), 1, 1)
        p_in = hop(p_top, 1, 0, (0, 1, 2, 3))
        near_late = after(near, p_in[0])
        _, wide_high = stage(
            ("enc", "dec"), 1, True,
            [(h_in, 0, 0), (h_two, 0, 2), (near_late, 0, 1), (near_late, half, 3)],
            [], weights, {}, (), wide_rows,
        )
        _, wide_low = stage(
            ("enc",), 0, True,
            [(packed, 0, 0), (packed_two, 0, 2), (near_late, 0, 1), (near_late, 2 * half, 3)],
            [], weights, {}, (), wide_rows,
        )
        _, wide_low = stage(
            ("dec", "decb"), 0, True,
            [(d_in, 0, 0), (d_two, 0, 2), (d_near, 0, 1), (d_near, half, 3)],
            [
                (packed, half, 0), (packed_two, half, 2),
                (near_late, half, 1), (near_late, 3 * half, 3),
            ],
            weights, wide_low, (), wide_rows,
        )
        _, wide_high = stage(
            ("decb", "encb"), 1, True,
            [(q_in, 0, 0), (q_two, 0, 2), (q_near, 0, 1), (q_near, half, 3)],
            [], weights, wide_high,
            {name: wide_low[name] for name in ("p_own", "p_send")}, wide_rows,
        )
        _, wide = stage(
            ("encb",), 0, True, [(p_in[flip], 0, flip) for flip in range(dp_count)],
            [], weights, wide_low,
            {name: wide_high[name] for name in ("e_own", "e_send")}, wide_rows,
        )
        wide["p_own"], wide["p_send"] = wide_high["p_own"], after(wide_high["p_send"], *p_in[1:])
    else:
        x0, cot = my_rows(inputs), my_rows(cotangent)
        wd_other = swap(wd)
        weights = {"we": load_other(load_own(we), we_other), "wd": load_other(load_own(wd), wd_other)}
        my_pair = lax.div(lax.axis_index("section"), 2)
        visits = [("enc", k) for k in range(pairs)]
        visits += [("dec", k) for k in reversed(range(pairs))]
        visits += [("decb", k) for k in range(pairs)]
        visits += [("encb", k) for k in reversed(range(pairs))]
        chain, wide = [{} for _ in range(pairs)], {}
        arrived = x0
        for i, (op, k) in enumerate(visits):
            entry = arrived if i % pairs == 0 else jnp.where(my_pair == k, arrived, entry)
            if i % pairs == pairs - 1:
                _, wide = stage(
                    (op,), None, True, [(over_dp(entry), 0, None)], [], weights, wide, (),
                    half * dp_count,
                )
            if i == len(visits) - 1:
                break
            x_out, chain[k] = stage((op,), k, False, [(arrived, 0, None)], [], weights, chain[k])
            target = visits[i + 1][1]
            if visits[i + 1] == ("decb", 0):
                arrived = cot
            elif target == k:
                arrived = x_out
            else:
                (arrived,) = hop(x_out, k, target)
    narrow = channels // dp_count
    p_own, p_oth = wide["p_own"], swap(wide["p_send"])
    e_own, e_oth = wide["e_own"], swap(wide["e_send"])
    dec_grads = wgrad(
        "wgrad_dec", narrow, 2 * narrow, 3 * narrow, channels, p_own, p_oth, p_own, p_oth
    )
    enc_grads = wgrad("wgrad_enc", 0, narrow, 0, channels, p_own, p_oth, e_own, e_oth)
    return (enc_grads[None], dec_grads[None])


def solution(mesh):
    in_specs = (
        P(None, ("group", "dp"), None),
        P(None, ("group", "dp"), None),
        P("section", None, None),
        P("section", None, None),
    )
    out_specs = (P(("group", "section"), "dp", None), P(("group", "section"), "dp", None))
    return jax.shard_map(body, mesh=mesh, in_specs=in_specs, out_specs=out_specs, check_vma=False)
```

```python
import functools

import jax
import jax.numpy as jnp
from jax import lax
from jax.experimental import pallas as pl
from jax.experimental.pallas import tpu as pltpu
from jax.sharding import PartitionSpec as P

EPS = 1e-06
TILE = 256
VMEM_LIMIT = 22 * 1024 * 1024
WIDE_LIMIT = 40 * 1024 * 1024


def dot(left, right):
    return lax.dot_general(
        left, right, (((1,), (0,)), ((), ())), preferred_element_type=jnp.float32
    )


def dot_t(left, right):
    return lax.dot_general(
        left, right, (((1,), (1,)), ((), ())), preferred_element_type=jnp.float32
    )


def dot_rows(left, right):
    return lax.dot_general(
        left, right, (((0,), (0,)), ((), ())), preferred_element_type=jnp.float32
    )


NEEDS = {
    "enc": (),
    "dec": ("n",),
    "decb": ("n", "r", "nd", "rd", "gb"),
    "encb": ("n", "r", "ga", "k"),
}
MAKES = {
    "enc": ("n", "r", "ga"),
    "dec": ("nd", "rd", "gb"),
    "decb": ("k",),
    "encb": (),
}
VMEM = pl.BlockSpec(memory_space=pltpu.VMEM)
ANY = pl.BlockSpec(memory_space=pl.ANY)


def own_kernel(own, both, sem):
    core = lax.rem(lax.axis_index("section"), 2)
    copy = pltpu.make_async_copy(own, both.at[core], sem)
    copy.start()
    copy.wait()


def other_kernel(before, other, both, sem):
    core = lax.rem(lax.axis_index("section"), 2)
    copy = pltpu.make_async_copy(other, both.at[1 - core], sem)
    copy.start()
    copy.wait()


def load_own(own):
    return pl.pallas_call(
        own_kernel,
        name="load_own",
        out_shape=jax.ShapeDtypeStruct((2,) + own.shape, own.dtype),
        in_specs=[pl.BlockSpec(memory_space=pltpu.HBM)],
        out_specs=VMEM,
        scratch_shapes=[pltpu.SemaphoreType.DMA],
        compiler_params=pltpu.CompilerParams(vmem_limit_bytes=VMEM_LIMIT),
    )(own)


def load_other(both, other):
    return pl.pallas_call(
        other_kernel,
        name="load_other",
        out_shape=jax.ShapeDtypeStruct(both.shape, both.dtype),
        in_specs=[VMEM, ANY],
        out_specs=VMEM,
        input_output_aliases={0: 0},
        scratch_shapes=[pltpu.SemaphoreType.DMA],
        compiler_params=pltpu.CompilerParams(vmem_limit_bytes=VMEM_LIMIT),
    )(both, other)


def stage_kernel(cfg, *refs):
    ops, pair, wide, dp_count = cfg["ops"], cfg["pair"], cfg["wide"], cfg["dp_count"]
    ref = dict(zip(cfg["names"], refs))
    section = lax.axis_index("section")
    core = lax.rem(section, 2)
    dp = lax.axis_index("dp")
    x = ref["out_x"] if "out_x" in ref else ref["work_x"]
    ybuf = ref.get("ybuf")
    rows, channels = x.shape
    tile_count = channels // TILE
    skip_k = cfg["skip_k"]

    def for_tiles(step, carry=0):
        def run(j, carry):
            at = j * TILE
            if not isinstance(j, int):
                at = pl.multiple_of(at, TILE)
            return step(at, pl.ds(at, TILE), carry)

        if cfg["unroll"]:
            for j in range(tile_count):
                carry = run(j, carry)
            return carry
        return lax.fori_loop(0, tile_count, run, carry)

    def by_core(level, name, cols, value):
        @pl.when(core == level)
        def _():
            ref[name + "_own"][:, cols] = value

        @pl.when(core != level)
        def _():
            ref[name + "_send"][:, cols] = value

    def normalize(level, n_ref, r_ref):
        values = x[...].astype(jnp.float32)
        inv = lax.rsqrt(jnp.mean(values * values, axis=-1, keepdims=True) + EPS)
        n_ref[level] = (values * inv).astype(jnp.bfloat16)
        r_ref[level] = jnp.broadcast_to(inv, (rows, 128))

    def activate(pre, gain_ref, level, sl):
        sigma = jax.nn.sigmoid(pre)
        gain_ref[level, :, sl] = sigma * (1.0 + pre * (1.0 - sigma))
        x[:, sl] = (x[:, sl].astype(jnp.float32) + pre * sigma).astype(jnp.bfloat16)

    def enc_level(level):
        n, we = ref["n"], ref["we"]
        normalize(level, n, ref["r"])

        def step(at, sl, carry):
            activate(dot(n[level], we[level, :, sl]), ref["ga"], level, sl)
            return carry

        for_tiles(step)

    def dec_level(level):
        n, nd, wd = ref["n"], ref["nd"], ref["wd"]
        normalize(level, nd, ref["rd"])

        def step(at, sl, carry):
            pre = dot(nd[level], wd[level, :channels, sl]) + dot(n[level], wd[level, channels:, sl])
            activate(pre, ref["gb"], level, sl)
            return carry

        for_tiles(step)

    def back(grad_ref, level, w_ref, base, n_ref, finish):
        grad = grad_ref[level]

        def step(at, sl, total):
            part = dot_t(grad, w_ref[level, pl.ds(base + at, TILE), :])
            ybuf[:, sl] = part
            return total + jnp.sum(
                part * n_ref[level, :, sl].astype(jnp.float32), axis=-1, keepdims=True
            )

        total = for_tiles(step, jnp.zeros((rows, 1), jnp.float32)) / channels

        def close(at, sl, carry):
            finish(sl, ybuf[:, sl] - n_ref[level, :, sl].astype(jnp.float32) * total)
            return carry

        for_tiles(close)

    def decb_level(level):
        n, nd, wd, u = ref.get("n"), ref["nd"], ref["wd"], ref["u"]
        u[level] = (x[...].astype(jnp.float32) * ref["gb"][level]).astype(jnp.bfloat16)
        if wide:
            width = channels // dp_count
            half = dp_count // 2
            by_core(
                level, "p", pl.ds(0, width),
                n[level, :, pl.ds(pl.multiple_of(dp * width, 128), width)],
            )
            low = pl.multiple_of(jnp.minimum(dp, half - 1) * 2 * width, 128)
            high = pl.multiple_of(jnp.maximum(dp - half, 0) * 2 * width, 128)

            @pl.when(dp < half)
            def _():
                by_core(level, "p", pl.ds(width, 2 * width), nd[level, :, pl.ds(low, 2 * width)])

            @pl.when(dp >= half)
            def _():
                by_core(level, "p", pl.ds(width, 2 * width), n[level, :, pl.ds(high, 2 * width)])

            by_core(level, "p", pl.ds(3 * width, channels), u[level])
        rd = ref["rd"][level, :, :1]

        def finish(sl, value):
            x[:, sl] = (x[:, sl].astype(jnp.float32) + rd * value).astype(jnp.bfloat16)

        if not (wide and level == 1 and ops[-1] == "decb"):
            back(u, level, wd, 0, nd, finish)
        if not skip_k:
            r, k = ref["r"][level, :, :1], ref["k"]

            def finish_skip(sl, value):
                k[level, :, sl] = (r * value).astype(jnp.bfloat16)

            back(u, level, wd, channels, n, finish_skip)

    def encb_level(level):
        n, we, e, k = ref["n"], ref["we"], ref["e"], ref["k"]
        e[level] = (x[...].astype(jnp.float32) * ref["ga"][level]).astype(jnp.bfloat16)
        if wide:
            by_core(level, "e", slice(None), e[level])
        if wide and level == 0:
            return
        r = ref["r"][level, :, :1]

        def finish(sl, value):
            x[:, sl] = (
                x[:, sl].astype(jnp.float32) + r * value + k[level, :, sl].astype(jnp.float32)
            ).astype(jnp.bfloat16)

        back(e, level, we, 0, n, finish)

    def fill(layout):
        for name, offset, flip in layout:
            source = ref[name]
            if flip is None:
                x[...] = source[offset : offset + rows]
            else:
                size = rows // dp_count
                at = pl.multiple_of(lax.bitwise_xor(dp, flip) * size, size)
                x[pl.ds(at, size)] = source[offset : offset + size]

    def run_live():
        fill(cfg["x_layout"])
        for op in ops:
            if op == "enc":
                enc_level(0)
                enc_level(1)
            if op == "dec":
                dec_level(1)
                dec_level(0)
            if op == "decb":
                if "dec" in ops:
                    fill(cfg["q_layout"])
                decb_level(0)
                decb_level(1)
            if op == "encb":
                encb_level(1)
                encb_level(0)

    if pair is None:
        run_live()
    else:
        here = lax.div(section, 2) == pair
        pl.when(here)(run_live)
        if cfg["prior"]:

            @pl.when(jnp.logical_not(here))
            def _():
                for name in cfg["prior"]:
                    ref[name][...] = ref["prior_" + name][...]


def run_stage(ops, pair, wide, unroll, rows, xs, qs, weights, state, dp_count, prior=()):
    channels = xs[0][0].shape[1]
    skip_k = pair == 0 and not wide
    bf16, f32 = jnp.bfloat16, jnp.float32
    matrix, pile = ((rows, channels), bf16), ((2, rows, channels), bf16)
    kinds = {
        "n": pile, "nd": pile, "k": pile, "u": pile, "e": pile,
        "r": ((2, rows, 128), f32), "rd": ((2, rows, 128), f32),
        "ga": ((2, rows, channels), f32), "gb": ((2, rows, channels), f32),
        "p": ((rows, channels + 3 * channels // dp_count), bf16),
    }
    names, args = [], []

    def operands(blocks):
        layout = []
        for value, offset, flip in blocks:
            known = [i for i, arg in enumerate(args) if arg is value]
            if known:
                name = names[known[0]]
            else:
                name = "x%d" % len(args)
                names.append(name)
                args.append(value)
            layout.append((name, offset, flip))
        return tuple(layout)

    x_layout = operands(xs)
    q_layout = operands(qs) if "dec" in ops and "decb" in ops else ()
    for kind, users in (("we", ("enc", "encb")), ("wd", ("dec", "decb"))):
        if any(op in users for op in ops):
            names.append(kind)
            args.append(weights[kind])
    made = set()
    for op in ops:
        for name in NEEDS[op]:
            if name not in made and name not in names and not (skip_k and op == "decb" and name in ("n", "r")):
                names.append(name)
                args.append(state[name])
        made.update(MAKES[op])
    for name in prior:
        names.append("prior_" + name)
        args.append(prior[name])
    in_count = len(args)
    outs, scratch = [], {}
    if not wide:
        outs.append(("out_x", matrix))
    else:
        scratch["work_x"] = matrix
    for op in ops:
        for name in MAKES[op]:
            if name == "k" and skip_k:
                continue
            if (name == "k" and "encb" in ops) or (name in ("nd", "rd", "gb") and "decb" in ops):
                scratch[name] = kinds[name]
            else:
                outs.append((name, kinds[name]))
        if op == "decb":
            scratch["u"] = pile
            if wide:
                outs += [("p_own", kinds["p"]), ("p_send", kinds["p"])]
        if op == "encb":
            scratch["e"] = pile
            if wide:
                outs += [("e_own", matrix), ("e_send", matrix)]
    if "decb" in ops or "encb" in ops:
        scratch["ybuf"] = ((rows, channels), f32)
    names += [o[0] for o in outs] + list(scratch)
    cfg = dict(
        ops=ops, pair=pair, wide=wide, names=names, dp_count=dp_count, skip_k=skip_k,
        unroll=unroll, prior=tuple(prior), x_layout=x_layout, q_layout=q_layout,
    )
    results = pl.pallas_call(
        functools.partial(stage_kernel, cfg),
        name=("wide_" if wide else "chain_") + "_".join(ops),
        out_shape=[jax.ShapeDtypeStruct(*o[1]) for o in outs],
        in_specs=[VMEM] * in_count,
        out_specs=[VMEM] * len(outs),
        scratch_shapes=[pltpu.VMEM(*v) for v in scratch.values()],
        compiler_params=pltpu.CompilerParams(
            vmem_limit_bytes=VMEM_LIMIT if unroll else WIDE_LIMIT
        ),
        cost_estimate=pl.CostEstimate(
            flops=1024, bytes_accessed=1024, transcendentals=0,
        ),
    )(*args)
    made = {name: value for (name, _), value in zip(outs, results)}
    x_out = made.pop("out_x", None)
    return x_out, {**state, **made}


def wgrad_kernel(skip, base, a_own, a_oth, b_own, b_oth, out, buf, sems):
    width, channels = buf.shape
    copies = []
    for index in range(channels // TILE):
        at = index * TILE
        total = dot_rows(a_own[:, skip : skip + width], b_own[:, base + at : base + at + TILE])
        total += dot_rows(a_oth[:, skip : skip + width], b_oth[:, base + at : base + at + TILE])
        buf[:, at : at + TILE] = total
        copy = pltpu.make_async_copy(
            buf.at[:, pl.ds(at, TILE)], out.at[:, pl.ds(at, TILE)], sems.at[index]
        )
        copy.start()
        copies.append(copy)
    for copy in copies:
        copy.wait()


def wgrad(name, skip, width, base, channels, a_own, a_oth, b_own, b_oth):
    return pl.pallas_call(
        functools.partial(wgrad_kernel, skip, base),
        name=name,
        out_shape=jax.ShapeDtypeStruct((width, channels), jnp.float32),
        in_specs=[VMEM] * 4,
        out_specs=ANY,
        scratch_shapes=[
            pltpu.VMEM((width, channels), jnp.float32),
            pltpu.SemaphoreType.DMA((channels // TILE,)),
        ],
        compiler_params=pltpu.CompilerParams(vmem_limit_bytes=VMEM_LIMIT),
        cost_estimate=pl.CostEstimate(
            flops=1024, bytes_accessed=1024, transcendentals=0,
        ),
    )(a_own, a_oth, b_own, b_oth)


def pack_kernel(inputs, cotangent, out, sems):
    core = lax.rem(lax.axis_index("section"), 2)
    count, row_count = inputs.shape[0] // 2, inputs.shape[1]
    copies = []
    for index, source in enumerate((inputs, cotangent)):
        for b in range(count):
            slot = index * count + b
            copies.append(
                pltpu.make_async_copy(
                    source.at[core * count + b],
                    out.at[pl.ds(slot * row_count, row_count)],
                    sems.at[slot],
                )
            )
            copies[-1].start()
    for copy in copies:
        copy.wait()


def pack(inputs, cotangent):
    batches, row_count, channels = inputs.shape
    return pl.pallas_call(
        pack_kernel,
        name="pack",
        out_shape=jax.ShapeDtypeStruct((batches * row_count, channels), inputs.dtype),
        in_specs=[pl.BlockSpec(memory_space=pltpu.HBM)] * 2,
        out_specs=VMEM,
        scratch_shapes=[pltpu.SemaphoreType.DMA((batches,))],
        compiler_params=pltpu.CompilerParams(vmem_limit_bytes=VMEM_LIMIT),
    )(inputs, cotangent)


def merge_kernel(low_count, *refs):
    pair = lax.div(lax.axis_index("section"), 2)
    out = refs[-1]
    for index, sources in enumerate((refs[:low_count], refs[low_count:-1])):

        @pl.when(pair == index)
        def _():
            at = 0
            for source in sources:
                size = source.shape[0]
                out[at : at + size] = source[...]
                at += size


def merge(low, high):
    rows = sum(value.shape[0] for value in low)
    return pl.pallas_call(
        functools.partial(merge_kernel, len(low)),
        name="merge",
        out_shape=jax.ShapeDtypeStruct((rows, low[0].shape[1]), low[0].dtype),
        in_specs=[VMEM] * (len(low) + len(high)),
        out_specs=VMEM,
        compiler_params=pltpu.CompilerParams(vmem_limit_bytes=VMEM_LIMIT),
    )(*low, *high)


def after(value, *others):
    return lax.optimization_barrier((value,) + others)[0]


def body(inputs, cotangent, enc_weights, dec_weights):
    section_count = lax.axis_size("section")
    dp_count = lax.axis_size("dp")
    core = lax.rem(lax.axis_index("section"), 2)
    pairs = section_count // 2
    batches, row_count, channels = inputs.shape
    half = batches * row_count // 2

    def my_rows(values):
        flat = values.reshape(2, half, channels)
        return lax.dynamic_index_in_dim(flat, core, 0, keepdims=False)

    def swap(value):
        return lax.ppermute(value, "section", [(i, i ^ 1) for i in range(section_count)])

    def flip_dp(value, flip, only=None):
        if only is None:
            return lax.ppermute(value, "dp", [(i, i ^ flip) for i in range(dp_count)])
        first = 2 * only * dp_count
        return lax.ppermute(
            value, ("section", "dp"), [(first + i, first + (i ^ flip)) for i in range(2 * dp_count)]
        )

    def over_dp(value):
        return lax.all_gather(value, "dp", axis=0, tiled=True)

    def hop(value, source, target, flips=(0,)):
        return [
            lax.ppermute(
                value,
                ("section", "dp"),
                [
                    ((2 * source + c) * dp_count + d, (2 * target + c) * dp_count + (d ^ flip))
                    for c in range(2)
                    for d in range(dp_count)
                ],
            )
            for flip in flips
        ]

    we, wd = enc_weights[0], dec_weights[0]
    we_other = swap(we)

    def stage(ops, k, wide, xs, qs, weights, state, prior=(), rows=half):
        return run_stage(
            ops, k, wide, pairs <= 2, rows, xs, qs, weights, state, dp_count, prior
        )

    if pairs == 2 and dp_count == 4:
        wide_rows = half * dp_count
        packed = pack(inputs, cotangent)
        packed_two = flip_dp(packed, 2, 0)
        we_own = load_own(we)
        wd_other = swap(after(wd, we_other, packed, we_own))
        weights = {"we": load_other(we_own, we_other), "wd": load_other(load_own(wd), wd_other)}
        h_top, low = stage(("enc",), 0, False, [(packed, 0, None)], [], weights, {})
        (h_in,) = hop(h_top, 0, 1)
        h_two = flip_dp(h_in, 2, 1)
        d_top, high = stage(("enc", "dec"), 1, False, [(h_in, 0, None)], [], weights, {})
        d_in, d_two = hop(d_top, 1, 0, (0, 2))
        q_top, low = stage(
            ("dec", "decb"), 0, False, [(d_in, 0, None)], [(packed, half, None)], weights, low
        )
        near = flip_dp(
            merge([packed, after(packed_two, q_top)], [h_in, after(h_two, q_top), h_in, h_two]), 1
        )
        q_in, q_two = hop(q_top, 0, 1, (0, 2))
        d_both = merge([d_in, d_two], [d_in, d_two])
        p_top, high = stage(
            ("decb", "encb"), 1, False, [(after(q_in, d_both), 0, None)], [], weights, high
        )
        p_in = hop(p_top, 1, 0, (0, 1, 2, 3))
        near_late = after(near, p_in[0])
        near_two = flip_dp(merge([after(d_both, p_in[0])], [q_in, after(q_two, p_in[0])]), 1)
        _, wide_high = stage(
            ("enc", "dec"), 1, True,
            [(h_in, 0, 0), (h_two, 0, 2), (near_late, 0, 1), (near_late, half, 3)],
            [], weights, {}, (), wide_rows,
        )
        _, wide_low = stage(
            ("enc",), 0, True,
            [(packed, 0, 0), (packed_two, 0, 2), (near_late, 0, 1), (near_late, 2 * half, 3)],
            [], weights, {}, (), wide_rows,
        )
        _, wide_low = stage(
            ("dec", "decb"), 0, True,
            [(d_in, 0, 0), (d_two, 0, 2), (near_two, 0, 1), (near_two, half, 3)],
            [
                (packed, half, 0), (packed_two, half, 2),
                (near_late, half, 1), (near_late, 3 * half, 3),
            ],
            weights, wide_low, (), wide_rows,
        )
        _, wide_high = stage(
            ("decb", "encb"), 1, True,
            [(q_in, 0, 0), (q_two, 0, 2), (near_two, 0, 1), (near_two, half, 3)],
            [], weights, wide_high,
            {name: wide_low[name] for name in ("p_own", "p_send")}, wide_rows,
        )
        _, wide = stage(
            ("encb",), 0, True, [(p_in[flip], 0, flip) for flip in range(dp_count)],
            [], weights, wide_low,
            {name: wide_high[name] for name in ("e_own", "e_send")}, wide_rows,
        )
        wide["p_own"], wide["p_send"] = wide_high["p_own"], after(wide_high["p_send"], *p_in[1:])
    else:
        x0, cot = my_rows(inputs), my_rows(cotangent)
        wd_other = swap(wd)
        weights = {"we": load_other(load_own(we), we_other), "wd": load_other(load_own(wd), wd_other)}
        my_pair = lax.div(lax.axis_index("section"), 2)
        visits = [("enc", k) for k in range(pairs)]
        visits += [("dec", k) for k in reversed(range(pairs))]
        visits += [("decb", k) for k in range(pairs)]
        visits += [("encb", k) for k in reversed(range(pairs))]
        chain, wide = [{} for _ in range(pairs)], {}
        arrived = x0
        for i, (op, k) in enumerate(visits):
            entry = arrived if i % pairs == 0 else jnp.where(my_pair == k, arrived, entry)
            if i % pairs == pairs - 1:
                _, wide = stage(
                    (op,), None, True, [(over_dp(entry), 0, None)], [], weights, wide, (),
                    half * dp_count,
                )
            if i == len(visits) - 1:
                break
            x_out, chain[k] = stage((op,), k, False, [(arrived, 0, None)], [], weights, chain[k])
            target = visits[i + 1][1]
            if visits[i + 1] == ("decb", 0):
                arrived = cot
            elif target == k:
                arrived = x_out
            else:
                (arrived,) = hop(x_out, k, target)
    narrow = channels // dp_count
    p_own, p_oth = wide["p_own"], swap(wide["p_send"])
    e_own, e_oth = wide["e_own"], swap(wide["e_send"])
    dec_grads = wgrad(
        "wgrad_dec", narrow, 2 * narrow, 3 * narrow, channels, p_own, p_oth, p_own, p_oth
    )
    enc_grads = wgrad("wgrad_enc", 0, narrow, 0, channels, p_own, p_oth, e_own, e_oth)
    return (enc_grads[None], dec_grads[None])


def solution(mesh):
    in_specs = (
        P(None, ("group", "dp"), None),
        P(None, ("group", "dp"), None),
        P("section", None, None),
        P("section", None, None),
    )
    out_specs = (P(("group", "section"), "dp", None), P(("group", "section"), "dp", None))
    return jax.shard_map(body, mesh=mesh, in_specs=in_specs, out_specs=out_specs, check_vma=False)
```

```python
import functools

import jax
import jax.numpy as jnp
from jax import lax
from jax.experimental import pallas as pl
from jax.experimental.pallas import tpu as pltpu
from jax.sharding import PartitionSpec as P

EPS = 1e-06
COSTS = {(('decb', 'encb'), False): 10000000000, (('dec', 'decb'), False): 10000000000}
TILE = 256
VMEM_LIMIT = 22 * 1024 * 1024
WIDE_LIMIT = 40 * 1024 * 1024


def dot(left, right):
    return lax.dot_general(
        left, right, (((1,), (0,)), ((), ())), preferred_element_type=jnp.float32
    )


def dot_t(left, right):
    return lax.dot_general(
        left, right, (((1,), (1,)), ((), ())), preferred_element_type=jnp.float32
    )


def dot_rows(left, right):
    return lax.dot_general(
        left, right, (((0,), (0,)), ((), ())), preferred_element_type=jnp.float32
    )


NEEDS = {
    "enc": (),
    "dec": ("n",),
    "decb": ("n", "r", "nd", "rd", "gb"),
    "encb": ("n", "r", "ga", "k"),
}
MAKES = {
    "enc": ("n", "r", "ga"),
    "dec": ("nd", "rd", "gb"),
    "decb": ("k",),
    "encb": (),
}
VMEM = pl.BlockSpec(memory_space=pltpu.VMEM)
ANY = pl.BlockSpec(memory_space=pl.ANY)


def own_kernel(own, both, sem):
    core = lax.rem(lax.axis_index("section"), 2)
    copy = pltpu.make_async_copy(own, both.at[core], sem)
    copy.start()
    copy.wait()


def other_kernel(before, other, both, sem):
    core = lax.rem(lax.axis_index("section"), 2)
    copy = pltpu.make_async_copy(other, both.at[1 - core], sem)
    copy.start()
    copy.wait()


def load_own(own):
    return pl.pallas_call(
        own_kernel,
        name="load_own",
        out_shape=jax.ShapeDtypeStruct((2,) + own.shape, own.dtype),
        in_specs=[pl.BlockSpec(memory_space=pltpu.HBM)],
        out_specs=VMEM,
        scratch_shapes=[pltpu.SemaphoreType.DMA],
        compiler_params=pltpu.CompilerParams(vmem_limit_bytes=VMEM_LIMIT),
    )(own)


def load_other(both, other):
    return pl.pallas_call(
        other_kernel,
        name="load_other",
        out_shape=jax.ShapeDtypeStruct(both.shape, both.dtype),
        in_specs=[VMEM, ANY],
        out_specs=VMEM,
        input_output_aliases={0: 0},
        scratch_shapes=[pltpu.SemaphoreType.DMA],
        compiler_params=pltpu.CompilerParams(vmem_limit_bytes=VMEM_LIMIT),
    )(both, other)


def stage_kernel(cfg, *refs):
    ops, pair, wide, dp_count = cfg["ops"], cfg["pair"], cfg["wide"], cfg["dp_count"]
    ref = dict(zip(cfg["names"], refs))
    section = lax.axis_index("section")
    core = lax.rem(section, 2)
    dp = lax.axis_index("dp")
    x = ref["out_x"] if "out_x" in ref else ref["work_x"]
    ybuf = ref.get("ybuf")
    rows, channels = x.shape
    tile_count = channels // TILE
    skip_k = cfg["skip_k"]

    def for_tiles(step, carry=0):
        def run(j, carry):
            at = j * TILE
            if not isinstance(j, int):
                at = pl.multiple_of(at, TILE)
            return step(at, pl.ds(at, TILE), carry)

        if cfg["unroll"]:
            for j in range(tile_count):
                carry = run(j, carry)
            return carry
        return lax.fori_loop(0, tile_count, run, carry)

    def by_core(level, name, cols, value):
        @pl.when(core == level)
        def _():
            ref[name + "_own"][:, cols] = value

        @pl.when(core != level)
        def _():
            ref[name + "_send"][:, cols] = value

    def normalize(level, n_ref, r_ref):
        values = x[...].astype(jnp.float32)
        inv = lax.rsqrt(jnp.mean(values * values, axis=-1, keepdims=True) + EPS)
        n_ref[level] = (values * inv).astype(jnp.bfloat16)
        r_ref[level] = jnp.broadcast_to(inv, (rows, 128))

    def activate(pre, gain_ref, level, sl):
        sigma = jax.nn.sigmoid(pre)
        gain_ref[level, :, sl] = sigma * (1.0 + pre * (1.0 - sigma))
        x[:, sl] = (x[:, sl].astype(jnp.float32) + pre * sigma).astype(jnp.bfloat16)

    def enc_level(level):
        n, we = ref["n"], ref["we"]
        normalize(level, n, ref["r"])

        def step(at, sl, carry):
            activate(dot(n[level], we[level, :, sl]), ref["ga"], level, sl)
            return carry

        for_tiles(step)

    def dec_level(level):
        n, nd, wd = ref["n"], ref["nd"], ref["wd"]
        normalize(level, nd, ref["rd"])

        def step(at, sl, carry):
            pre = dot(nd[level], wd[level, :channels, sl]) + dot(n[level], wd[level, channels:, sl])
            activate(pre, ref["gb"], level, sl)
            return carry

        for_tiles(step)

    def back(grad_ref, level, w_ref, base, n_ref, finish):
        grad = grad_ref[level]

        def step(at, sl, total):
            part = dot_t(grad, w_ref[level, pl.ds(base + at, TILE), :])
            ybuf[:, sl] = part
            return total + jnp.sum(
                part * n_ref[level, :, sl].astype(jnp.float32), axis=-1, keepdims=True
            )

        total = for_tiles(step, jnp.zeros((rows, 1), jnp.float32)) / channels

        def close(at, sl, carry):
            finish(sl, ybuf[:, sl] - n_ref[level, :, sl].astype(jnp.float32) * total)
            return carry

        for_tiles(close)

    def decb_level(level):
        n, nd, wd, u = ref.get("n"), ref["nd"], ref["wd"], ref["u"]
        u[level] = (x[...].astype(jnp.float32) * ref["gb"][level]).astype(jnp.bfloat16)
        if wide:
            width = channels // dp_count
            half = dp_count // 2
            by_core(
                level, "p", pl.ds(0, width),
                n[level, :, pl.ds(pl.multiple_of(dp * width, 128), width)],
            )
            low = pl.multiple_of(jnp.minimum(dp, half - 1) * 2 * width, 128)
            high = pl.multiple_of(jnp.maximum(dp - half, 0) * 2 * width, 128)

            @pl.when(dp < half)
            def _():
                by_core(level, "p", pl.ds(width, 2 * width), nd[level, :, pl.ds(low, 2 * width)])

            @pl.when(dp >= half)
            def _():
                by_core(level, "p", pl.ds(width, 2 * width), n[level, :, pl.ds(high, 2 * width)])

            by_core(level, "p", pl.ds(3 * width, channels), u[level])
        rd = ref["rd"][level, :, :1]

        def finish(sl, value):
            x[:, sl] = (x[:, sl].astype(jnp.float32) + rd * value).astype(jnp.bfloat16)

        if not (wide and level == 1 and ops[-1] == "decb"):
            back(u, level, wd, 0, nd, finish)
        if not skip_k and not (wide and level == 0):
            r, k = ref["r"][level, :, :1], ref["k"]

            def finish_skip(sl, value):
                k[level, :, sl] = (r * value).astype(jnp.bfloat16)

            back(u, level, wd, channels, n, finish_skip)

    def encb_level(level):
        n, we, e, k = ref["n"], ref["we"], ref["e"], ref["k"]
        e[level] = (x[...].astype(jnp.float32) * ref["ga"][level]).astype(jnp.bfloat16)
        if wide:
            by_core(level, "e", slice(None), e[level])
        if wide and level == 0:
            return
        r = ref["r"][level, :, :1]

        def finish(sl, value):
            x[:, sl] = (
                x[:, sl].astype(jnp.float32) + r * value + k[level, :, sl].astype(jnp.float32)
            ).astype(jnp.bfloat16)

        back(e, level, we, 0, n, finish)

    def fill(layout):
        for name, offset, flip in layout:
            source = ref[name]
            if flip is None:
                x[...] = source[offset : offset + rows]
            else:
                size = rows // dp_count
                at = pl.multiple_of(lax.bitwise_xor(dp, flip) * size, size)
                x[pl.ds(at, size)] = source[offset : offset + size]

    def run_live():
        fill(cfg["x_layout"])
        for op in ops:
            if op == "enc":
                enc_level(0)
                enc_level(1)
            if op == "dec":
                dec_level(1)
                dec_level(0)
            if op == "decb":
                if "dec" in ops:
                    fill(cfg["q_layout"])
                decb_level(0)
                decb_level(1)
            if op == "encb":
                encb_level(1)
                encb_level(0)

    if pair is None:
        run_live()
    else:
        here = lax.div(section, 2) == pair
        pl.when(here)(run_live)
        if cfg["prior"]:

            @pl.when(jnp.logical_not(here))
            def _():
                for name in cfg["prior"]:
                    ref[name][...] = ref["prior_" + name][...]


def run_stage(ops, pair, wide, unroll, rows, xs, qs, weights, state, dp_count, prior=()):
    channels = xs[0][0].shape[1]
    skip_k = pair == 0 and not wide
    bf16, f32 = jnp.bfloat16, jnp.float32
    matrix, pile = ((rows, channels), bf16), ((2, rows, channels), bf16)
    kinds = {
        "n": pile, "nd": pile, "k": pile, "u": pile, "e": pile,
        "r": ((2, rows, 128), f32), "rd": ((2, rows, 128), f32),
        "ga": ((2, rows, channels), f32), "gb": ((2, rows, channels), f32),
        "p": ((rows, channels + 3 * channels // dp_count), bf16),
    }
    names, args = [], []

    def operands(blocks):
        layout = []
        for value, offset, flip in blocks:
            known = [i for i, arg in enumerate(args) if arg is value]
            if known:
                name = names[known[0]]
            else:
                name = "x%d" % len(args)
                names.append(name)
                args.append(value)
            layout.append((name, offset, flip))
        return tuple(layout)

    x_layout = operands(xs)
    q_layout = operands(qs) if "dec" in ops and "decb" in ops else ()
    for kind, users in (("we", ("enc", "encb")), ("wd", ("dec", "decb"))):
        if any(op in users for op in ops):
            names.append(kind)
            args.append(weights[kind])
    made = set()
    for op in ops:
        for name in NEEDS[op]:
            if name not in made and name not in names and not (skip_k and op == "decb" and name in ("n", "r")):
                names.append(name)
                args.append(state[name])
        made.update(MAKES[op])
    for name in prior:
        names.append("prior_" + name)
        args.append(prior[name])
    in_count = len(args)
    outs, scratch = [], {}
    if not wide:
        outs.append(("out_x", matrix))
    else:
        scratch["work_x"] = matrix
    for op in ops:
        for name in MAKES[op]:
            if name == "k" and skip_k:
                continue
            if (name == "k" and "encb" in ops) or (name in ("nd", "rd", "gb") and "decb" in ops):
                scratch[name] = kinds[name]
            else:
                outs.append((name, kinds[name]))
        if op == "decb":
            scratch["u"] = pile
            if wide:
                outs += [("p_own", kinds["p"]), ("p_send", kinds["p"])]
        if op == "encb":
            scratch["e"] = pile
            if wide:
                outs += [("e_own", matrix), ("e_send", matrix)]
    if "decb" in ops or "encb" in ops:
        scratch["ybuf"] = ((rows, channels), f32)
    names += [o[0] for o in outs] + list(scratch)
    cfg = dict(
        ops=ops, pair=pair, wide=wide, names=names, dp_count=dp_count, skip_k=skip_k,
        unroll=unroll, prior=tuple(prior), x_layout=x_layout, q_layout=q_layout,
    )
    results = pl.pallas_call(
        functools.partial(stage_kernel, cfg),
        name=("wide_" if wide else "chain_") + "_".join(ops),
        out_shape=[jax.ShapeDtypeStruct(*o[1]) for o in outs],
        in_specs=[VMEM] * in_count,
        out_specs=[VMEM] * len(outs),
        scratch_shapes=[pltpu.VMEM(*v) for v in scratch.values()],
        compiler_params=pltpu.CompilerParams(
            vmem_limit_bytes=VMEM_LIMIT if unroll else WIDE_LIMIT
        ),
        cost_estimate=pl.CostEstimate(
            flops=COSTS.get((ops, wide), 1024), bytes_accessed=1024, transcendentals=0,
        ),
    )(*args)
    made = {name: value for (name, _), value in zip(outs, results)}
    x_out = made.pop("out_x", None)
    return x_out, {**state, **made}


def wgrad_kernel(skip, base, a_own, a_oth, b_own, b_oth, out, buf, sems):
    width, channels = buf.shape
    copies = []
    for index in range(channels // TILE):
        at = index * TILE
        total = dot_rows(a_own[:, skip : skip + width], b_own[:, base + at : base + at + TILE])
        total += dot_rows(a_oth[:, skip : skip + width], b_oth[:, base + at : base + at + TILE])
        buf[:, at : at + TILE] = total
        copy = pltpu.make_async_copy(
            buf.at[:, pl.ds(at, TILE)], out.at[:, pl.ds(at, TILE)], sems.at[index]
        )
        copy.start()
        copies.append(copy)
    for copy in copies:
        copy.wait()


def wgrad(name, skip, width, base, channels, a_own, a_oth, b_own, b_oth):
    return pl.pallas_call(
        functools.partial(wgrad_kernel, skip, base),
        name=name,
        out_shape=jax.ShapeDtypeStruct((width, channels), jnp.float32),
        in_specs=[VMEM] * 4,
        out_specs=ANY,
        scratch_shapes=[
            pltpu.VMEM((width, channels), jnp.float32),
            pltpu.SemaphoreType.DMA((channels // TILE,)),
        ],
        compiler_params=pltpu.CompilerParams(vmem_limit_bytes=VMEM_LIMIT),
        cost_estimate=pl.CostEstimate(
            flops=1024, bytes_accessed=1024, transcendentals=0,
        ),
    )(a_own, a_oth, b_own, b_oth)


def pack_kernel(inputs, cotangent, out, sems):
    core = lax.rem(lax.axis_index("section"), 2)
    count, row_count = inputs.shape[0] // 2, inputs.shape[1]
    copies = []
    for index, source in enumerate((inputs, cotangent)):
        for b in range(count):
            slot = index * count + b
            copies.append(
                pltpu.make_async_copy(
                    source.at[core * count + b],
                    out.at[pl.ds(slot * row_count, row_count)],
                    sems.at[slot],
                )
            )
            copies[-1].start()
    for copy in copies:
        copy.wait()


def pack(inputs, cotangent):
    batches, row_count, channels = inputs.shape
    return pl.pallas_call(
        pack_kernel,
        name="pack",
        out_shape=jax.ShapeDtypeStruct((batches * row_count, channels), inputs.dtype),
        in_specs=[pl.BlockSpec(memory_space=pltpu.HBM)] * 2,
        out_specs=VMEM,
        scratch_shapes=[pltpu.SemaphoreType.DMA((batches,))],
        compiler_params=pltpu.CompilerParams(vmem_limit_bytes=VMEM_LIMIT),
    )(inputs, cotangent)


def merge_kernel(low_count, *refs):
    pair = lax.div(lax.axis_index("section"), 2)
    out = refs[-1]
    for index, sources in enumerate((refs[:low_count], refs[low_count:-1])):

        @pl.when(pair == index)
        def _():
            at = 0
            for source in sources:
                size = source.shape[0]
                out[at : at + size] = source[...]
                at += size


def merge(low, high):
    rows = sum(value.shape[0] for value in low)
    return pl.pallas_call(
        functools.partial(merge_kernel, len(low)),
        name="merge",
        out_shape=jax.ShapeDtypeStruct((rows, low[0].shape[1]), low[0].dtype),
        in_specs=[VMEM] * (len(low) + len(high)),
        out_specs=VMEM,
        compiler_params=pltpu.CompilerParams(vmem_limit_bytes=VMEM_LIMIT),
    )(*low, *high)


def after(value, *others):
    return lax.optimization_barrier((value,) + others)[0]


def body(inputs, cotangent, enc_weights, dec_weights):
    section_count = lax.axis_size("section")
    dp_count = lax.axis_size("dp")
    core = lax.rem(lax.axis_index("section"), 2)
    pairs = section_count // 2
    batches, row_count, channels = inputs.shape
    half = batches * row_count // 2

    def my_rows(values):
        flat = values.reshape(2, half, channels)
        return lax.dynamic_index_in_dim(flat, core, 0, keepdims=False)

    def swap(value):
        return lax.ppermute(value, "section", [(i, i ^ 1) for i in range(section_count)])

    def flip_dp(value, flip, only=None):
        if only is None:
            return lax.ppermute(value, "dp", [(i, i ^ flip) for i in range(dp_count)])
        first = 2 * only * dp_count
        return lax.ppermute(
            value, ("section", "dp"), [(first + i, first + (i ^ flip)) for i in range(2 * dp_count)]
        )

    def over_dp(value):
        return lax.all_gather(value, "dp", axis=0, tiled=True)

    def hop(value, source, target, flips=(0,)):
        return [
            lax.ppermute(
                value,
                ("section", "dp"),
                [
                    ((2 * source + c) * dp_count + d, (2 * target + c) * dp_count + (d ^ flip))
                    for c in range(2)
                    for d in range(dp_count)
                ],
            )
            for flip in flips
        ]

    we, wd = enc_weights[0], dec_weights[0]
    we_other = swap(we)

    def stage(ops, k, wide, xs, qs, weights, state, prior=(), rows=half):
        return run_stage(
            ops, k, wide, pairs <= 2, rows, xs, qs, weights, state, dp_count, prior
        )

    if pairs == 2 and dp_count == 4:
        wide_rows = half * dp_count
        packed = pack(inputs, cotangent)
        packed_two = flip_dp(packed, 2, 0)
        we_own = load_own(we)
        wd_other = swap(after(wd, we_other, packed, we_own))
        weights = {"we": load_other(we_own, we_other), "wd": load_other(load_own(wd), wd_other)}
        h_top, low = stage(("enc",), 0, False, [(packed, 0, None)], [], weights, {})
        (h_in,) = hop(h_top, 0, 1)
        h_two = flip_dp(h_in, 2, 1)
        d_top, high = stage(("enc", "dec"), 1, False, [(h_in, 0, None)], [], weights, {})
        d_in, d_two = hop(d_top, 1, 0, (0, 2))
        q_top, low = stage(
            ("dec", "decb"), 0, False, [(d_in, 0, None)], [(packed, half, None)], weights, low
        )
        q_in, q_two = hop(q_top, 0, 1, (0, 2))
        near = flip_dp(
            merge([packed, after(packed_two, q_in)], [h_in, after(h_two, q_in), h_in, h_two]), 1
        )
        d_both = merge([d_in, d_two], [d_in, d_two])
        p_top, high = stage(
            ("decb", "encb"), 1, False, [(q_in, 0, None)], [], weights, high
        )
        p_in = hop(p_top, 1, 0, (0, 1, 2, 3))
        near_late = after(near, p_in[0])
        near_two = flip_dp(merge([after(d_both, p_in[0])], [q_in, after(q_two, p_in[0])]), 1)
        _, wide_high = stage(
            ("enc", "dec"), 1, True,
            [(h_in, 0, 0), (h_two, 0, 2), (near_late, 0, 1), (near_late, half, 3)],
            [], weights, {}, (), wide_rows,
        )
        _, wide_low = stage(
            ("enc",), 0, True,
            [(packed, 0, 0), (packed_two, 0, 2), (near_late, 0, 1), (near_late, 2 * half, 3)],
            [], weights, {}, (), wide_rows,
        )
        _, wide_low = stage(
            ("dec", "decb"), 0, True,
            [(d_in, 0, 0), (d_two, 0, 2), (near_two, 0, 1), (near_two, half, 3)],
            [
                (packed, half, 0), (packed_two, half, 2),
                (near_late, half, 1), (near_late, 3 * half, 3),
            ],
            weights, wide_low, (), wide_rows,
        )
        _, wide_high = stage(
            ("decb", "encb"), 1, True,
            [(q_in, 0, 0), (q_two, 0, 2), (near_two, 0, 1), (near_two, half, 3)],
            [], weights, wide_high,
            {name: wide_low[name] for name in ("p_own", "p_send")}, wide_rows,
        )
        _, wide = stage(
            ("encb",), 0, True, [(p_in[flip], 0, flip) for flip in range(dp_count)],
            [], weights, wide_low,
            {name: wide_high[name] for name in ("e_own", "e_send")}, wide_rows,
        )
        wide["p_own"], wide["p_send"] = wide_high["p_own"], after(wide_high["p_send"], *p_in[1:])
    else:
        x0, cot = my_rows(inputs), my_rows(cotangent)
        wd_other = swap(wd)
        weights = {"we": load_other(load_own(we), we_other), "wd": load_other(load_own(wd), wd_other)}
        my_pair = lax.div(lax.axis_index("section"), 2)
        visits = [("enc", k) for k in range(pairs)]
        visits += [("dec", k) for k in reversed(range(pairs))]
        visits += [("decb", k) for k in range(pairs)]
        visits += [("encb", k) for k in reversed(range(pairs))]
        chain, wide = [{} for _ in range(pairs)], {}
        arrived = x0
        for i, (op, k) in enumerate(visits):
            entry = arrived if i % pairs == 0 else jnp.where(my_pair == k, arrived, entry)
            if i % pairs == pairs - 1:
                _, wide = stage(
                    (op,), None, True, [(over_dp(entry), 0, None)], [], weights, wide, (),
                    half * dp_count,
                )
            if i == len(visits) - 1:
                break
            x_out, chain[k] = stage((op,), k, False, [(arrived, 0, None)], [], weights, chain[k])
            target = visits[i + 1][1]
            if visits[i + 1] == ("decb", 0):
                arrived = cot
            elif target == k:
                arrived = x_out
            else:
                (arrived,) = hop(x_out, k, target)
    narrow = channels // dp_count
    p_own, p_oth = wide["p_own"], swap(wide["p_send"])
    e_own, e_oth = wide["e_own"], swap(wide["e_send"])
    dec_grads = wgrad(
        "wgrad_dec", narrow, 2 * narrow, 3 * narrow, channels, p_own, p_oth, p_own, p_oth
    )
    enc_grads = wgrad("wgrad_enc", 0, narrow, 0, channels, p_own, p_oth, e_own, e_oth)
    return (enc_grads[None], dec_grads[None])


def solution(mesh):
    in_specs = (
        P(None, ("group", "dp"), None),
        P(None, ("group", "dp"), None),
        P("section", None, None),
        P("section", None, None),
    )
    out_specs = (P(("group", "section"), "dp", None), P(("group", "section"), "dp", None))
    return jax.shard_map(body, mesh=mesh, in_specs=in_specs, out_specs=out_specs, check_vma=False)
```

```python
import functools

import jax
import jax.numpy as jnp
from jax import lax
from jax.experimental import pallas as pl
from jax.experimental.pallas import tpu as pltpu
from jax.sharding import PartitionSpec as P

EPS = 1e-06
COSTS = {(('decb', 'encb'), False): 10000000000, (('dec', 'decb'), False): 10000000000}
TILE = 256
VMEM_LIMIT = 22 * 1024 * 1024
WIDE_LIMIT = 40 * 1024 * 1024


def dot(left, right):
    return lax.dot_general(
        left, right, (((1,), (0,)), ((), ())), preferred_element_type=jnp.float32
    )


def dot_t(left, right):
    return lax.dot_general(
        left, right, (((1,), (1,)), ((), ())), preferred_element_type=jnp.float32
    )


def dot_rows(left, right):
    return lax.dot_general(
        left, right, (((0,), (0,)), ((), ())), preferred_element_type=jnp.float32
    )


NEEDS = {
    "enc": (),
    "dec": ("n",),
    "decb": ("n", "r", "nd", "rd", "gb"),
    "encb": ("n", "r", "ga", "k"),
}
MAKES = {
    "enc": ("n", "r", "ga"),
    "dec": ("nd", "rd", "gb"),
    "decb": ("k",),
    "encb": (),
}
VMEM = pl.BlockSpec(memory_space=pltpu.VMEM)
ANY = pl.BlockSpec(memory_space=pl.ANY)


def own_kernel(own, both, sem):
    core = lax.rem(lax.axis_index("section"), 2)
    copy = pltpu.make_async_copy(own, both.at[core], sem)
    copy.start()
    copy.wait()


def other_kernel(before, other, both, sem):
    core = lax.rem(lax.axis_index("section"), 2)
    copy = pltpu.make_async_copy(other, both.at[1 - core], sem)
    copy.start()
    copy.wait()


def load_own(own):
    return pl.pallas_call(
        own_kernel,
        name="load_own",
        out_shape=jax.ShapeDtypeStruct((2,) + own.shape, own.dtype),
        in_specs=[pl.BlockSpec(memory_space=pltpu.HBM)],
        out_specs=VMEM,
        scratch_shapes=[pltpu.SemaphoreType.DMA],
        compiler_params=pltpu.CompilerParams(vmem_limit_bytes=VMEM_LIMIT),
    )(own)


def load_other(both, other):
    return pl.pallas_call(
        other_kernel,
        name="load_other",
        out_shape=jax.ShapeDtypeStruct(both.shape, both.dtype),
        in_specs=[VMEM, ANY],
        out_specs=VMEM,
        input_output_aliases={0: 0},
        scratch_shapes=[pltpu.SemaphoreType.DMA],
        compiler_params=pltpu.CompilerParams(vmem_limit_bytes=VMEM_LIMIT),
    )(both, other)


def stage_kernel(cfg, *refs):
    ops, pair, wide, dp_count = cfg["ops"], cfg["pair"], cfg["wide"], cfg["dp_count"]
    ref = dict(zip(cfg["names"], refs))
    section = lax.axis_index("section")
    core = lax.rem(section, 2)
    dp = lax.axis_index("dp")
    x = ref["out_x"] if "out_x" in ref else ref["work_x"]
    ybuf = ref.get("ybuf")
    rows, channels = x.shape
    tile_count = channels // TILE
    skip_k = cfg["skip_k"]

    def for_tiles(step, carry=0):
        def run(j, carry):
            at = j * TILE
            if not isinstance(j, int):
                at = pl.multiple_of(at, TILE)
            return step(at, pl.ds(at, TILE), carry)

        if cfg["unroll"]:
            for j in range(tile_count):
                carry = run(j, carry)
            return carry
        return lax.fori_loop(0, tile_count, run, carry)

    def by_core(level, name, cols, value):
        @pl.when(core == level)
        def _():
            ref[name + "_own"][:, cols] = value

        @pl.when(core != level)
        def _():
            ref[name + "_send"][:, cols] = value

    def normalize(level, n_ref, r_ref):
        values = x[...].astype(jnp.float32)
        inv = lax.rsqrt(jnp.mean(values * values, axis=-1, keepdims=True) + EPS)
        n_ref[level] = (values * inv).astype(jnp.bfloat16)
        r_ref[level] = jnp.broadcast_to(inv, (rows, 128))

    def activate(pre, gain_ref, level, sl):
        sigma = jax.nn.sigmoid(pre)
        if gain_ref is not None:
            gain_ref[level, :, sl] = sigma * (1.0 + pre * (1.0 - sigma))
        x[:, sl] = (x[:, sl].astype(jnp.float32) + pre * sigma).astype(jnp.bfloat16)

    def enc_level(level):
        n, we = ref["n"], ref["we"]
        normalize(level, n, ref["r"])

        def step(at, sl, carry):
            activate(dot(n[level], we[level, :, sl]), ref.get("ga"), level, sl)
            return carry

        for_tiles(step)

    def dec_level(level):
        n, nd, wd = ref["n"], ref["nd"], ref["wd"]
        normalize(level, nd, ref["rd"])

        def step(at, sl, carry):
            pre = dot(nd[level], wd[level, :channels, sl]) + dot(n[level], wd[level, channels:, sl])
            activate(pre, ref["gb"], level, sl)
            return carry

        for_tiles(step)

    def back(grad_ref, level, w_ref, base, n_ref, finish):
        grad = grad_ref[level]

        def step(at, sl, total):
            part = dot_t(grad, w_ref[level, pl.ds(base + at, TILE), :])
            ybuf[:, sl] = part
            return total + jnp.sum(
                part * n_ref[level, :, sl].astype(jnp.float32), axis=-1, keepdims=True
            )

        total = for_tiles(step, jnp.zeros((rows, 1), jnp.float32)) / channels

        def close(at, sl, carry):
            finish(sl, ybuf[:, sl] - n_ref[level, :, sl].astype(jnp.float32) * total)
            return carry

        for_tiles(close)

    def decb_level(level):
        n, nd, wd, u = ref.get("n"), ref["nd"], ref["wd"], ref["u"]
        u[level] = (x[...].astype(jnp.float32) * ref["gb"][level]).astype(jnp.bfloat16)
        if wide:
            width = channels // dp_count
            half = dp_count // 2
            by_core(
                level, "p", pl.ds(0, width),
                n[level, :, pl.ds(pl.multiple_of(dp * width, 128), width)],
            )
            low = pl.multiple_of(jnp.minimum(dp, half - 1) * 2 * width, 128)
            high = pl.multiple_of(jnp.maximum(dp - half, 0) * 2 * width, 128)

            @pl.when(dp < half)
            def _():
                by_core(level, "p", pl.ds(width, 2 * width), nd[level, :, pl.ds(low, 2 * width)])

            @pl.when(dp >= half)
            def _():
                by_core(level, "p", pl.ds(width, 2 * width), n[level, :, pl.ds(high, 2 * width)])

            by_core(level, "p", pl.ds(3 * width, channels), u[level])
        rd = ref["rd"][level, :, :1]

        def finish(sl, value):
            x[:, sl] = (x[:, sl].astype(jnp.float32) + rd * value).astype(jnp.bfloat16)

        if not (wide and level == 1 and ops[-1] == "decb"):
            back(u, level, wd, 0, nd, finish)
        if not skip_k and not (wide and level == 0):
            r, k = ref["r"][level, :, :1], ref["k"]

            def finish_skip(sl, value):
                k[level, :, sl] = (r * value).astype(jnp.bfloat16)

            back(u, level, wd, channels, n, finish_skip)

    def encb_level(level):
        n, we, e, k = ref["n"], ref["we"], ref["e"], ref["k"]
        e[level] = (x[...].astype(jnp.float32) * ref["ga"][level]).astype(jnp.bfloat16)
        if wide:
            by_core(level, "e", slice(None), e[level])
        if wide and level == 0:
            return
        r = ref["r"][level, :, :1]

        def finish(sl, value):
            x[:, sl] = (
                x[:, sl].astype(jnp.float32) + r * value + k[level, :, sl].astype(jnp.float32)
            ).astype(jnp.bfloat16)

        back(e, level, we, 0, n, finish)

    def fill(layout):
        for name, offset, flip in layout:
            source = ref[name]
            if flip is None:
                x[...] = source[offset : offset + rows]
            else:
                size = rows // dp_count
                at = pl.multiple_of(lax.bitwise_xor(dp, flip) * size, size)
                x[pl.ds(at, size)] = source[offset : offset + size]

    def run_live():
        fill(cfg["x_layout"])
        for op in ops:
            if op == "enc":
                enc_level(0)
                enc_level(1)
            if op == "dec":
                dec_level(1)
                dec_level(0)
            if op == "decb":
                if "dec" in ops:
                    fill(cfg["q_layout"])
                decb_level(0)
                decb_level(1)
            if op == "encb":
                encb_level(1)
                encb_level(0)

    if pair is None:
        run_live()
    else:
        here = lax.div(section, 2) == pair
        pl.when(here)(run_live)
        if cfg["prior"]:

            @pl.when(jnp.logical_not(here))
            def _():
                for name in cfg["prior"]:
                    ref[name][...] = ref["prior_" + name][...]


def run_stage(ops, pair, wide, unroll, rows, xs, qs, weights, state, dp_count, prior=()):
    channels = xs[0][0].shape[1]
    skip_k = pair == 0 and not wide
    bf16, f32 = jnp.bfloat16, jnp.float32
    matrix, pile = ((rows, channels), bf16), ((2, rows, channels), bf16)
    kinds = {
        "n": pile, "nd": pile, "k": pile, "u": pile, "e": pile,
        "r": ((2, rows, 128), f32), "rd": ((2, rows, 128), f32),
        "ga": ((2, rows, channels), f32), "gb": ((2, rows, channels), f32),
        "p": ((rows, channels + 3 * channels // dp_count), bf16),
    }
    names, args = [], []

    def operands(blocks):
        layout = []
        for value, offset, flip in blocks:
            known = [i for i, arg in enumerate(args) if arg is value]
            if known:
                name = names[known[0]]
            else:
                name = "x%d" % len(args)
                names.append(name)
                args.append(value)
            layout.append((name, offset, flip))
        return tuple(layout)

    x_layout = operands(xs)
    q_layout = operands(qs) if "dec" in ops and "decb" in ops else ()
    for kind, users in (("we", ("enc", "encb")), ("wd", ("dec", "decb"))):
        if any(op in users for op in ops):
            names.append(kind)
            args.append(weights[kind])
    made = set()
    for op in ops:
        for name in NEEDS[op]:
            if name not in made and name not in names and not (skip_k and op == "decb" and name in ("n", "r")):
                names.append(name)
                args.append(state[name])
        made.update(MAKES[op])
    for name in prior:
        names.append("prior_" + name)
        args.append(prior[name])
    in_count = len(args)
    outs, scratch = [], {}
    if not wide:
        outs.append(("out_x", matrix))
    else:
        scratch["work_x"] = matrix
    for op in ops:
        for name in MAKES[op]:
            if name in ("k", "ga") and skip_k:
                continue
            if (name == "k" and "encb" in ops) or (name in ("nd", "rd", "gb") and "decb" in ops):
                scratch[name] = kinds[name]
            else:
                outs.append((name, kinds[name]))
        if op == "decb":
            scratch["u"] = pile
            if wide:
                outs += [("p_own", kinds["p"]), ("p_send", kinds["p"])]
        if op == "encb":
            scratch["e"] = pile
            if wide:
                outs += [("e_own", matrix), ("e_send", matrix)]
    if "decb" in ops or "encb" in ops:
        scratch["ybuf"] = ((rows, channels), f32)
    names += [o[0] for o in outs] + list(scratch)
    cfg = dict(
        ops=ops, pair=pair, wide=wide, names=names, dp_count=dp_count, skip_k=skip_k,
        unroll=unroll, prior=tuple(prior), x_layout=x_layout, q_layout=q_layout,
    )
    results = pl.pallas_call(
        functools.partial(stage_kernel, cfg),
        name=("wide_" if wide else "chain_") + "_".join(ops),
        out_shape=[jax.ShapeDtypeStruct(*o[1]) for o in outs],
        in_specs=[VMEM] * in_count,
        out_specs=[VMEM] * len(outs),
        scratch_shapes=[pltpu.VMEM(*v) for v in scratch.values()],
        compiler_params=pltpu.CompilerParams(
            vmem_limit_bytes=VMEM_LIMIT if unroll else WIDE_LIMIT
        ),
        cost_estimate=pl.CostEstimate(
            flops=COSTS.get((ops, wide), 1024), bytes_accessed=1024, transcendentals=0,
        ),
    )(*args)
    made = {name: value for (name, _), value in zip(outs, results)}
    x_out = made.pop("out_x", None)
    return x_out, {**state, **made}


def wgrad_kernel(skip, base, a_own, a_oth, b_own, b_oth, out, buf, sems):
    width, channels = buf.shape
    copies = []
    for index in range(channels // TILE):
        at = index * TILE
        total = dot_rows(a_own[:, skip : skip + width], b_own[:, base + at : base + at + TILE])
        total += dot_rows(a_oth[:, skip : skip + width], b_oth[:, base + at : base + at + TILE])
        buf[:, at : at + TILE] = total
        copy = pltpu.make_async_copy(
            buf.at[:, pl.ds(at, TILE)], out.at[:, pl.ds(at, TILE)], sems.at[index]
        )
        copy.start()
        copies.append(copy)
    for copy in copies:
        copy.wait()


def wgrad(name, skip, width, base, channels, a_own, a_oth, b_own, b_oth):
    return pl.pallas_call(
        functools.partial(wgrad_kernel, skip, base),
        name=name,
        out_shape=jax.ShapeDtypeStruct((width, channels), jnp.float32),
        in_specs=[VMEM] * 4,
        out_specs=ANY,
        scratch_shapes=[
            pltpu.VMEM((width, channels), jnp.float32),
            pltpu.SemaphoreType.DMA((channels // TILE,)),
        ],
        compiler_params=pltpu.CompilerParams(vmem_limit_bytes=VMEM_LIMIT),
        cost_estimate=pl.CostEstimate(
            flops=1024, bytes_accessed=1024, transcendentals=0,
        ),
    )(a_own, a_oth, b_own, b_oth)


def pack_kernel(inputs, cotangent, out, sems):
    core = lax.rem(lax.axis_index("section"), 2)
    count, row_count = inputs.shape[0] // 2, inputs.shape[1]
    copies = []
    for index, source in enumerate((inputs, cotangent)):
        for b in range(count):
            slot = index * count + b
            copies.append(
                pltpu.make_async_copy(
                    source.at[core * count + b],
                    out.at[pl.ds(slot * row_count, row_count)],
                    sems.at[slot],
                )
            )
            copies[-1].start()
    for copy in copies:
        copy.wait()


def pack(inputs, cotangent):
    batches, row_count, channels = inputs.shape
    return pl.pallas_call(
        pack_kernel,
        name="pack",
        out_shape=jax.ShapeDtypeStruct((batches * row_count, channels), inputs.dtype),
        in_specs=[pl.BlockSpec(memory_space=pltpu.HBM)] * 2,
        out_specs=VMEM,
        scratch_shapes=[pltpu.SemaphoreType.DMA((batches,))],
        compiler_params=pltpu.CompilerParams(vmem_limit_bytes=VMEM_LIMIT),
    )(inputs, cotangent)


def merge_kernel(low_count, *refs):
    pair = lax.div(lax.axis_index("section"), 2)
    out = refs[-1]
    for index, sources in enumerate((refs[:low_count], refs[low_count:-1])):

        @pl.when(pair == index)
        def _():
            at = 0
            for source in sources:
                size = source.shape[0]
                out[at : at + size] = source[...]
                at += size


def merge(low, high):
    rows = sum(value.shape[0] for value in low)
    return pl.pallas_call(
        functools.partial(merge_kernel, len(low)),
        name="merge",
        out_shape=jax.ShapeDtypeStruct((rows, low[0].shape[1]), low[0].dtype),
        in_specs=[VMEM] * (len(low) + len(high)),
        out_specs=VMEM,
        compiler_params=pltpu.CompilerParams(vmem_limit_bytes=VMEM_LIMIT),
    )(*low, *high)


def after(value, *others):
    return lax.optimization_barrier((value,) + others)[0]


def body(inputs, cotangent, enc_weights, dec_weights):
    section_count = lax.axis_size("section")
    dp_count = lax.axis_size("dp")
    core = lax.rem(lax.axis_index("section"), 2)
    pairs = section_count // 2
    batches, row_count, channels = inputs.shape
    half = batches * row_count // 2

    def my_rows(values):
        flat = values.reshape(2, half, channels)
        return lax.dynamic_index_in_dim(flat, core, 0, keepdims=False)

    def swap(value):
        return lax.ppermute(value, "section", [(i, i ^ 1) for i in range(section_count)])

    def flip_dp(value, flip, only=None):
        if only is None:
            return lax.ppermute(value, "dp", [(i, i ^ flip) for i in range(dp_count)])
        first = 2 * only * dp_count
        return lax.ppermute(
            value, ("section", "dp"), [(first + i, first + (i ^ flip)) for i in range(2 * dp_count)]
        )

    def over_dp(value):
        return lax.all_gather(value, "dp", axis=0, tiled=True)

    def hop(value, source, target, flips=(0,)):
        return [
            lax.ppermute(
                value,
                ("section", "dp"),
                [
                    ((2 * source + c) * dp_count + d, (2 * target + c) * dp_count + (d ^ flip))
                    for c in range(2)
                    for d in range(dp_count)
                ],
            )
            for flip in flips
        ]

    we, wd = enc_weights[0], dec_weights[0]
    we_other = swap(we)

    def stage(ops, k, wide, xs, qs, weights, state, prior=(), rows=half):
        return run_stage(
            ops, k, wide, pairs <= 2, rows, xs, qs, weights, state, dp_count, prior
        )

    if pairs == 2 and dp_count == 4:
        wide_rows = half * dp_count
        packed = pack(inputs, cotangent)
        packed_two = flip_dp(packed, 2, 0)
        we_own = load_own(we)
        wd_other = swap(after(wd, we_other, packed, we_own))
        weights = {"we": load_other(we_own, we_other), "wd": load_other(load_own(wd), wd_other)}
        h_top, low = stage(("enc",), 0, False, [(packed, 0, None)], [], weights, {})
        (h_in,) = hop(h_top, 0, 1)
        h_two = flip_dp(h_in, 2, 1)
        d_top, high = stage(("enc", "dec"), 1, False, [(h_in, 0, None)], [], weights, {})
        d_in, d_two = hop(d_top, 1, 0, (0, 2))
        q_top, low = stage(
            ("dec", "decb"), 0, False, [(d_in, 0, None)], [(packed, half, None)], weights, low
        )
        q_in, q_two = hop(q_top, 0, 1, (0, 2))
        near = flip_dp(
            merge([packed, after(packed_two, q_in)], [h_in, after(h_two, q_in), h_in, h_two]), 1
        )
        d_both = merge([d_in, d_two], [d_in, d_two])
        p_top, high = stage(
            ("decb", "encb"), 1, False, [(q_in, 0, None)], [], weights, high
        )
        p_in = hop(p_top, 1, 0, (0, 1, 2, 3))
        near_late = after(near, p_in[0])
        near_two = flip_dp(merge([after(d_both, p_in[0])], [q_in, after(q_two, p_in[0])]), 1)
        _, wide_high = stage(
            ("enc", "dec"), 1, True,
            [(h_in, 0, 0), (h_two, 0, 2), (near_late, 0, 1), (near_late, half, 3)],
            [], weights, {}, (), wide_rows,
        )
        _, wide_low = stage(
            ("enc",), 0, True,
            [(packed, 0, 0), (packed_two, 0, 2), (near_late, 0, 1), (near_late, 2 * half, 3)],
            [], weights, {}, (), wide_rows,
        )
        _, wide_low = stage(
            ("dec", "decb"), 0, True,
            [(d_in, 0, 0), (d_two, 0, 2), (near_two, 0, 1), (near_two, half, 3)],
            [
                (packed, half, 0), (packed_two, half, 2),
                (near_late, half, 1), (near_late, 3 * half, 3),
            ],
            weights, wide_low, (), wide_rows,
        )
        _, wide_high = stage(
            ("decb", "encb"), 1, True,
            [(q_in, 0, 0), (q_two, 0, 2), (near_two, 0, 1), (near_two, half, 3)],
            [], weights, wide_high,
            {name: wide_low[name] for name in ("p_own", "p_send")}, wide_rows,
        )
        _, wide = stage(
            ("encb",), 0, True, [(p_in[flip], 0, flip) for flip in range(dp_count)],
            [], weights, wide_low,
            {name: wide_high[name] for name in ("e_own", "e_send")}, wide_rows,
        )
        wide["p_own"], wide["p_send"] = wide_high["p_own"], after(wide_high["p_send"], *p_in[1:])
    else:
        x0, cot = my_rows(inputs), my_rows(cotangent)
        wd_other = swap(wd)
        weights = {"we": load_other(load_own(we), we_other), "wd": load_other(load_own(wd), wd_other)}
        my_pair = lax.div(lax.axis_index("section"), 2)
        visits = [("enc", k) for k in range(pairs)]
        visits += [("dec", k) for k in reversed(range(pairs))]
        visits += [("decb", k) for k in range(pairs)]
        visits += [("encb", k) for k in reversed(range(pairs))]
        chain, wide = [{} for _ in range(pairs)], {}
        arrived = x0
        for i, (op, k) in enumerate(visits):
            entry = arrived if i % pairs == 0 else jnp.where(my_pair == k, arrived, entry)
            if i % pairs == pairs - 1:
                _, wide = stage(
                    (op,), None, True, [(over_dp(entry), 0, None)], [], weights, wide, (),
                    half * dp_count,
                )
            if i == len(visits) - 1:
                break
            x_out, chain[k] = stage((op,), k, False, [(arrived, 0, None)], [], weights, chain[k])
            target = visits[i + 1][1]
            if visits[i + 1] == ("decb", 0):
                arrived = cot
            elif target == k:
                arrived = x_out
            else:
                (arrived,) = hop(x_out, k, target)
    narrow = channels // dp_count
    p_own, p_oth = wide["p_own"], swap(wide["p_send"])
    e_own, e_oth = wide["e_own"], swap(wide["e_send"])
    dec_grads = wgrad(
        "wgrad_dec", narrow, 2 * narrow, 3 * narrow, channels, p_own, p_oth, p_own, p_oth
    )
    enc_grads = wgrad("wgrad_enc", 0, narrow, 0, channels, p_own, p_oth, e_own, e_oth)
    return (enc_grads[None], dec_grads[None])


def solution(mesh):
    in_specs = (
        P(None, ("group", "dp"), None),
        P(None, ("group", "dp"), None),
        P("section", None, None),
        P("section", None, None),
    )
    out_specs = (P(("group", "section"), "dp", None), P(("group", "section"), "dp", None))
    return jax.shard_map(body, mesh=mesh, in_specs=in_specs, out_specs=out_specs, check_vma=False)
```
